32 devices in a mesh: tm: 8 (over y, x, core), space: 4 (over z).
Axes of the slice: x: 2, y: 2, z: 4, core: 2. Of those that a mesh axis runs over, the one named last changes fastest.
Arguments:
- point_states: float32 [8, 128, 1024], P('tm', 'space'), may hold values from -6 to 6
- initial_state: float32 [128, 1024], P('space'), may hold values from -6 to 6
- node_rate: float32 [128, 1024], P('space'), may hold values from 0.01 to 0.06
- source_map: float32 [128, 1024], P('space'), may hold values from -6 to 6
- waveform: float32 [128], replicated, may hold values from -2 to 2
- cond_table: float32 [16], replicated, may hold values from 0.25 to 4
- class_map: int32 [16, 8], P('space'), may hold values from 0 to 15
- interval_steps: int32 [8], replicated, may hold values from 1 to 20, 128 in all
Outputs:
- corrected: float32 [8, 128, 1024], P('tm', 'space')
The draws below stay inside these ranges and needn't reach their ends.
Inputs may be any that keep to these rules, and one draw needn't show every extreme that they name: `interval_steps`: they sum to 128 and the largest equals 20.
All inputs are finite; a program needn't handle non-finite values.
Results may differ from the reference program's by a relative error of at most 0.0003.
Values sent between devices are 32-bit elements; how exact they have to be, the bound alone decides.
No kernel may reach another device: no remote copies, remote signals or barrier semaphores. Data moves between devices by JAX's collectives and lax.ppermute only.
A program may use at most 64 MiB of HBM per device.

```python
import math
import jax
import jax.numpy as jnp
import numpy as np
from jax import lax

NY = 1024
STEP_MOST = 20
CSUB = 5
CLASSES = 16
BLK_R = 8
BLK_C = 128
NX = 128
NCP = 8
NT = 128


def plant(result, key, low, high):
    longest = result.shape.index(max(result.shape))
    spots = []
    for shift in (0, 1):
        where = [jax.random.randint(jax.random.fold_in(key, axis), (), 0, length) for axis, length in enumerate(result.shape)]
        where[longest] = (where[longest] + shift) % result.shape[longest]
        spots.append(tuple(where))
    return result.at[spots[0]].set(low).at[spots[1]].set(high)


def block_scale(key, shape, split, least, high):
    loudness = 1.0
    for axis_at, blocks in split:
        heights = jax.random.uniform(jax.random.fold_in(jax.random.fold_in(key, 6), axis_at), (blocks,), jnp.float32, least / len(split), high / len(split))
        loudness = loudness * jnp.repeat(jnp.exp(heights), shape[axis_at] // blocks).reshape((-1,) + (1,) * (len(shape) - 1 - axis_at))
    return loudness


def profile(number_of, total, limit, lean):
    loads = [(1 << 20) // math.isqrt(rank ** lean) + 1 for rank in range(2, number_of + 1)]
    rest, given = total - limit - (number_of - 1), [1] * (number_of - 1)
    while rest > 0:
        free = [i for i in range(number_of - 1) if given[i] < limit]
        mass, remaining = sum([loads[i] for i in free]), rest
        for i in free:
            addition = min(limit - given[i], max(1, remaining * loads[i] // mass), rest)
            given[i] = given[i] + addition
            rest = rest - addition
    return np.array([limit] + given)


def uneven_parts(rng, count, total, reach, lean):
    if count == 2:
        one = jax.random.randint(rng, (), max(1, total - reach), min(reach, total - 1) + 1)
        return jnp.stack([one, total - one])
    lengths = jnp.asarray(profile(count, total, reach, lean), jnp.int32)
    twos = (count - 1) // 2
    donor, receiver = lengths[1:1 + 2 * twos:2], lengths[2:2 + 2 * twos:2]
    room = jnp.minimum(donor - 1, reach - receiver)
    moved = jax.random.randint(jax.random.fold_in(rng, 1), (twos,), 0, 1 << 20) % (room + 1)
    lengths = lengths.at[1:1 + 2 * twos:2].set(donor - moved).at[2:2 + 2 * twos:2].set(receiver + moved)
    return lengths[jax.random.permutation(jax.random.fold_in(rng, 2), count)]


def bell_draw(own_key, extent, spread, reach, cuts=(), kind=jnp.bfloat16):
    values = jax.random.normal(own_key, extent, jnp.float32) * spread
    if len(cuts) > 0:
        values = block_scale(own_key, extent, cuts, -0.22, 0.18) * values
    return jnp.clip(values, min=-reach, max=reach).astype(kind)


def setup_inputs(seed: int = 0) -> dict:
    streams_of = jax.random.split(jax.random.key(seed), 9)
    return {
        "point_states": bell_draw(streams_of[0], (NCP, NX, NY), 1.0, 6.0, ((0, 8), (1, 4)), jnp.float32),
        "initial_state": bell_draw(streams_of[1], (NX, NY), 1.0, 6.0, ((0, 4),), jnp.float32),
        "node_rate": jnp.clip(jnp.exp(math.log(0.06) - 1.7917595 * jax.random.uniform(streams_of[2], (NX, NY), jnp.float32) ** block_scale(streams_of[2], (NX, NY), ((0, 4),), -0.2, 0.2)), 0.01, 0.06),
        "source_map": bell_draw(streams_of[3], (NX, NY), 1.0, 6.0, ((0, 4),), jnp.float32),
        "waveform": bell_draw(streams_of[4], (NT,), 0.3, 2.0, (), jnp.float32),
        "cond_table": jnp.clip(jnp.exp(jax.random.uniform(streams_of[5], (CLASSES,), jnp.float32, math.log(0.25), math.log(4.0))), 0.25, 4.0),
        "class_map": plant(jax.random.randint(streams_of[6], (NX // BLK_R, NY // BLK_C), 0, CLASSES), jax.random.fold_in(streams_of[6], 1), 0, CLASSES - 1).astype(jnp.int32),
        "interval_steps": uneven_parts(streams_of[7], NCP, NT, STEP_MOST, 2).astype(jnp.int32),
    }


def neighbours(values):
    zero_row = jnp.zeros_like(values[..., :1, :])
    zero_col = jnp.zeros_like(values[..., :, :1])
    above_row = jnp.concatenate([zero_row, values[..., :-1, :]], axis=-2)
    below_row = jnp.concatenate([values[..., 1:, :], zero_row], axis=-2)
    left_col = jnp.concatenate([zero_col, values[..., :, :-1]], axis=-1)
    right_col = jnp.concatenate([values[..., :, 1:], zero_col], axis=-1)
    return (above_row, below_row, left_col, right_col)

def restrict(values):
    return 0.25 * (values[..., 0::2, 0::2] + values[..., 1::2, 0::2] + (values[..., 0::2, 1::2] + values[..., 1::2, 1::2]))

def prolong(values):
    return jnp.repeat(jnp.repeat(values, 2, axis=-2), 2, axis=-1)

def node_conductance(class_map, cond_table):
    classes = jnp.arange(cond_table.shape[0], dtype=jnp.int32)
    picked = lax.optimization_barrier(jnp.sum(jnp.where(class_map[None] == classes[:, None, None], cond_table[:, None, None], 0.0), axis=0))
    return jnp.repeat(jnp.repeat(picked, BLK_R, axis=0), BLK_C, axis=1)

def base_weights(rates, conduct):
    above_row, below_row, left_col, right_col = neighbours(conduct)
    return (rates * jnp.sqrt(conduct * above_row), rates * jnp.sqrt(conduct * below_row), rates * jnp.sqrt(conduct * left_col), rates * jnp.sqrt(conduct * right_col))

def combine(state_now, above_row, below_row, left_col, right_col, weights, forcing):
    to_above, to_below, to_left, to_right = weights
    return state_now + (to_above * (above_row - state_now) + to_below * (below_row - state_now) + to_left * (left_col - state_now) + to_right * (right_col - state_now)) + forcing

def coarse_step(carried, coarse_weights, factor):
    to_above, to_below, to_left, to_right = coarse_weights
    above_row, below_row, left_col, right_col = neighbours(carried)
    return carried + factor * (to_above * (above_row - carried) + to_below * (below_row - carried) + to_left * (left_col - carried) + to_right * (right_col - carried))

def reference(point_states, initial_state, node_rate, source_map, waveform, cond_table, class_map, interval_steps):
    conduct = node_conductance(class_map, cond_table)
    weights = base_weights(node_rate, conduct)
    coarse_weights = base_weights(restrict(node_rate), restrict(conduct))
    starts = (jnp.cumsum(interval_steps) - interval_steps).astype(jnp.int32)

    def propagate(element):
        state_in, first_step, step_count = element

        def advance(fine_step, state_now):
            above_row, below_row, left_col, right_col = neighbours(state_now)
            forcing = waveform[first_step + fine_step] * source_map
            updated = combine(state_now, above_row, below_row, left_col, right_col, weights, forcing)
            return jnp.where(fine_step < step_count, updated, state_now)
        return lax.fori_loop(0, STEP_MOST, advance, state_in)
    first_pass = lax.map(propagate, (point_states, starts, interval_steps))
    relaxed = jnp.concatenate([initial_state[None], first_pass[:-1]], axis=0)
    second_pass = lax.map(propagate, (relaxed, starts, interval_steps))
    change = restrict(second_pass - first_pass)
    coarse_res = jnp.concatenate([jnp.zeros_like(change[:1]), change[:-1]], axis=0)
    factors = interval_steps.astype(jnp.float32) / (4.0 * CSUB)

    def link(carry, link_item):
        residue, factor = link_item
        error_now = carry + residue
        carried = error_now
        for substep in range(CSUB):
            carried = coarse_step(carried, coarse_weights, factor)
        return (carried, error_now)
    unused, errors = lax.scan(link, jnp.zeros_like(coarse_res[0]), (coarse_res, factors))
    return relaxed + prolong(errors)
```

```python
import functools

import jax
import jax.numpy as jnp
from jax import lax
from jax.experimental import pallas as pl
from jax.experimental.pallas import tpu as pltpu
from jax.sharding import PartitionSpec as P

STEP_MOST = 20
CSUB = 5
BLK_R = 8
BLK_C = 128
SUB = 8
LANES = 128
MAIN = STEP_MOST // SUB * SUB
REST = STEP_MOST - MAIN
HALO = -(-STEP_MOST // SUB) * SUB
HT = HALO // SUB
PAD = SUB
VM = pl.BlockSpec(memory_space=pltpu.VMEM)
SM = pl.BlockSpec(memory_space=pltpu.SMEM)
F32 = jnp.float32


def f32(*shape):
    return jax.ShapeDtypeStruct(shape, F32)


def call(body, ins, outs, scratch, flops):
    return pl.pallas_call(
        body,
        out_shape=outs,
        in_specs=ins,
        out_specs=jax.tree.map(lambda _: VM, outs),
        scratch_shapes=scratch,
        cost_estimate=pl.CostEstimate(flops=flops, bytes_accessed=1 << 20, transcendentals=0),
    )


def iota(axis, shape=(SUB, LANES)):
    return lax.broadcasted_iota(jnp.int32, shape, axis)


def cols(c):
    return slice(c * LANES, (c + 1) * LANES)


def beside(tiles, c, left_edge=None):
    lane = iota(1)
    before = pltpu.roll(tiles[c], 1, 1)
    after = pltpu.roll(tiles[c], LANES - 1, 1)
    if c > 0:
        before = jnp.where(lane == 0, pltpu.roll(tiles[c - 1], 1, 1), before)
    elif left_edge is not None:
        before = jnp.where(lane == 0, left_edge, before)
    if c + 1 < len(tiles):
        after = jnp.where(lane == LANES - 1, pltpu.roll(tiles[c + 1], LANES - 1, 1), after)
    elif left_edge is not None:
        after = jnp.where(lane == LANES - 1, left_edge, after)
    return before, after


def halve():
    wide, narrow = iota(0, (2 * LANES, LANES)), iota(1, (2 * LANES, LANES))
    return jnp.where(wide // 2 == narrow, 1.0, 0.0).astype(F32)


def double():
    narrow, wide = iota(0, (LANES, 2 * LANES)), iota(1, (LANES, 2 * LANES))
    return jnp.where(wide // 2 == narrow, 1.0, 0.0).astype(F32)


def dot(a, b):
    return jnp.dot(a, b, precision=lax.Precision.HIGHEST, preferred_element_type=F32)


def row_pairs(ref, index, first, rows):
    top = ref[(*index, pl.ds(first, rows, stride=2), slice(None))]
    return top + ref[(*index, pl.ds(first + 1, rows, stride=2), slice(None))]


def pack_body(point, rate, source, table, classes, pay_a, pay_b, coarse, tmp):
    rows, width = point.shape
    blocks, tiles = rows // BLK_R, width // LANES
    odd = lax.rem(lax.axis_index("space"), 2) == 1

    def fill(out, high):
        main = rows - MAIN if high else 0
        rest = rows - MAIN - REST if high else MAIN
        for i, ref in enumerate((point, rate, source)):
            out[i * MAIN : (i + 1) * MAIN, :] = ref[main : main + MAIN, :]
            at = 3 * MAIN + i * REST
            out[at : at + REST, :] = ref[rest : rest + REST, :]
        first = blocks - HT if high else 0
        for b in range(HT):
            for c in range(tiles):
                value = table[classes[first + b, c]]
                at = 3 * MAIN + 3 * REST + b
                out[at : at + 1, cols(c)] = jnp.full((1, LANES), value, F32)

    @pl.when(odd)
    def _():
        fill(pay_a, False)
        fill(pay_b, True)

    @pl.when(jnp.logical_not(odd))
    def _():
        fill(pay_a, True)
        fill(pay_b, False)

    for c in range(tiles):
        tmp[c, :, :] = rate[:, cols(c)]
    pairs = halve()
    for c in range(tiles // 2):
        wide = jnp.concatenate([row_pairs(tmp, (2 * c + k,), 0, rows // 2) for k in (0, 1)], axis=1)
        coarse[: rows // 2, cols(c)] = 0.25 * dot(wide, pairs)
        for b in range(blocks):
            halves = [jnp.full((1, LANES), table[classes[b, 2 * c + k]], F32) for k in (0, 1)]
            at = rows // 2 + b
            coarse[at : at + 1, cols(c)] = jnp.where(iota(1, (1, LANES)) < LANES // 2, halves[0], halves[1])


def sweep(state, weights, force, count, tiles, strip_tiles, wave):
    def step(t, reach):
        now = lax.rem(t, 2)
        amount = None if wave is None else wave(t)
        for r in range(HT - reach, HT + strip_tiles + reach):
            at = PAD + r * SUB
            here = [state[now, c, at : at + SUB, :] for c in range(tiles)]
            for c in range(tiles):
                left, right = beside(here, c)
                above = state[now, c, at - 1 : at + SUB - 1, :]
                below = state[now, c, at + 1 : at + SUB + 1, :]
                w = [weights[k, c, r * SUB : (r + 1) * SUB, :] for k in range(5)]
                new = (w[0] * here[c] + w[1] * above) + (w[2] * below + w[3] * left) + w[4] * right
                if amount is not None:
                    new = new + amount * force[c, r * SUB : (r + 1) * SUB, :]
                state[1 - now, c, at : at + SUB, :] = new

    begin = 0
    for reach in range(HT, -1, -1):
        if reach == HT:
            steps = jnp.maximum(count - 1 - SUB * (HT - 1), 0)
        elif reach > 0:
            steps = jnp.clip(count - 1 - SUB * (reach - 1), 0, SUB)
        else:
            steps = 1
        lax.fori_loop(begin, begin + steps, lambda t, _, reach=reach: step(t, reach), None)
        begin = begin + steps
    return lax.rem(count, 2)


def with_halos(odd, got_a, got_b, place):
    @pl.when(odd)
    def _():
        place(got_a, True)
        place(got_b, False)

    @pl.when(jnp.logical_not(odd))
    def _():
        place(got_b, True)
        place(got_a, False)


def unpack(out, lead, tiles, rows, payload, above, which, at=0):
    for c in range(tiles):
        if above:
            main, rest = at + HALO - MAIN, at + HALO - MAIN - REST
        else:
            main, rest = at + HALO + rows, at + HALO + rows + MAIN
        first = 3 * MAIN + which * REST
        out[(*lead, c, slice(main, main + MAIN), slice(None))] = payload[which * MAIN : (which + 1) * MAIN, cols(c)]
        out[(*lead, c, slice(rest, rest + REST), slice(None))] = payload[first : first + REST, cols(c)]


def first_body(
    point, rate, source, got_a, got_b, initial, table, classes, steps, waveform,
    relaxed, edge_a, edge_b, weights, state, force, rates, conduct,
):
    rows, width = point.shape
    tiles, strip_tiles, blocks = width // LANES, rows // SUB, rows // BLK_R
    mine, strip = lax.axis_index("tm"), lax.axis_index("space")
    odd = lax.rem(strip, 2) == 1
    start = lax.fori_loop(0, mine, lambda i, total: total + steps[i], jnp.int32(0))
    count = steps[mine]

    for c in range(tiles):
        for r in range(strip_tiles):
            at, to = slice(r * SUB, (r + 1) * SUB), slice(HALO + r * SUB, HALO + (r + 1) * SUB)
            state[0, c, PAD + HALO + r * SUB : PAD + HALO + (r + 1) * SUB, :] = point[at, cols(c)]
            rates[c, to, :] = rate[at, cols(c)]
            force[c, to, :] = source[at, cols(c)]
        for b in range(blocks):
            at = PAD + HALO + b * BLK_R
            conduct[c, at : at + BLK_R, :] = jnp.full((BLK_R, LANES), table[classes[b, c]], F32)
        zero = jnp.zeros((SUB, LANES), F32)
        conduct[c, 0:PAD, :] = zero
        conduct[c, PAD + 2 * HALO + rows :, :] = zero
        for at in (0, HALO + rows + HALO - SUB):
            rates[c, at : at + SUB, :] = zero
            force[c, at : at + SUB, :] = zero
            state[0, c, PAD + at : PAD + at + SUB, :] = zero

    def place(payload, above):
        unpack(state, (0,), tiles, rows, payload, above, 0, PAD)
        unpack(rates, (), tiles, rows, payload, above, 1)
        unpack(force, (), tiles, rows, payload, above, 2)
        for b in range(HT):
            at = PAD + b * BLK_R + (0 if above else HALO + rows)
            row = 3 * MAIN + 3 * REST + b
            for c in range(tiles):
                conduct[c, at : at + BLK_R, :] = jnp.broadcast_to(payload[row : row + 1, cols(c)], (BLK_R, LANES))

    with_halos(odd, got_a, got_b, place)

    zero = jnp.zeros((SUB, LANES), F32)
    for r in range(2 * HT + strip_tiles):
        at = PAD + r * SUB
        here = [conduct[c, at : at + SUB, :] for c in range(tiles)]
        for c in range(tiles):
            left, right = beside(here, c, zero)
            above = conduct[c, at - 1 : at + SUB - 1, :]
            below = conduct[c, at + 1 : at + SUB + 1, :]
            own = rates[c, r * SUB : (r + 1) * SUB, :]
            w = [own * jnp.sqrt(here[c] * other) for other in (above, below, left, right)]
            weights[0, c, r * SUB : (r + 1) * SUB, :] = 1.0 - (((w[0] + w[1]) + w[2]) + w[3])
            for k in range(4):
                weights[k + 1, c, r * SUB : (r + 1) * SUB, :] = w[k]

    now = sweep(state, weights, force, count, tiles, strip_tiles, lambda t: waveform[start + t])

    def give(read):
        for c in range(tiles):
            for r in range(strip_tiles):
                relaxed[r * SUB : (r + 1) * SUB, cols(c)] = read(r, c)

        @pl.when(odd)
        def _():
            for c in range(tiles):
                for r in range(HT):
                    edge_a[r * SUB : (r + 1) * SUB, cols(c)] = read(r, c)
                    edge_b[r * SUB : (r + 1) * SUB, cols(c)] = read(strip_tiles - HT + r, c)

        @pl.when(jnp.logical_not(odd))
        def _():
            for c in range(tiles):
                for r in range(HT):
                    edge_b[r * SUB : (r + 1) * SUB, cols(c)] = read(r, c)
                    edge_a[r * SUB : (r + 1) * SUB, cols(c)] = read(strip_tiles - HT + r, c)

    last = mine == lax.axis_size("tm") - 1

    @pl.when(last)
    def _():
        give(lambda r, c: initial[r * SUB : (r + 1) * SUB, cols(c)])

    @pl.when(jnp.logical_not(last))
    def _():
        give(lambda r, c: state[now, c, pl.ds(PAD + HALO + r * SUB, SUB), :])


def second_body(relaxed, edge_a, edge_b, point, got_a, got_b, weights, steps, coarse, state, tmp):
    rows, width = point.shape
    tiles, strip_tiles = width // LANES, rows // SUB
    mine, strip = lax.axis_index("tm"), lax.axis_index("space")
    odd = lax.rem(strip, 2) == 1
    count = steps[mine]
    for c in range(tiles):
        for r in range(strip_tiles):
            at = slice(r * SUB, (r + 1) * SUB)
            to = PAD + HALO + r * SUB
            state[0, c, to : to + SUB, :] = relaxed[at, cols(c)] - point[at, cols(c)]
        for at in (0, HALO + rows + HALO - SUB):
            tmp[c, at : at + SUB, :] = jnp.zeros((SUB, LANES), F32)

    def place(pair, above):
        edge, payload = pair
        unpack(tmp, (), tiles, rows, payload, above, 0)
        base = 0 if above else HALO + rows
        for c in range(tiles):
            for r in range(HT):
                at = base + r * SUB
                state[0, c, PAD + at : PAD + at + SUB, :] = edge[r * SUB : (r + 1) * SUB, cols(c)] - tmp[c, at : at + SUB, :]

    with_halos(odd, (edge_a, got_a), (edge_b, got_b), place)
    now = sweep(state, weights, None, count, tiles, strip_tiles, None)
    pairs = halve()
    for c in range(tiles // 2):
        wide = [row_pairs(state, (now, 2 * c + k), PAD + HALO, rows // 2) for k in (0, 1)]
        coarse[:, cols(c)] = 0.25 * dot(jnp.concatenate(wide, axis=1), pairs)


def assemble_body(strips, fields, total, weights, conduct):
    count = len(strips)
    rows, width = strips[0].shape
    tiles = width // LANES
    mine = lax.axis_index("space")
    per_block = BLK_R // 2
    zero = jnp.zeros((SUB, LANES), F32)
    for c in range(tiles):
        conduct[c, 0:PAD, :] = zero
        conduct[c, PAD + count * rows :, :] = zero
    for k in range(count):
        base = (mine ^ k) * rows
        for c in range(tiles):
            for r in range(rows // SUB):
                to = pl.multiple_of(base + r * SUB, SUB)
                total[c, pl.ds(to, SUB), :] = strips[k][r * SUB : (r + 1) * SUB, cols(c)]
                weights[0, c, pl.ds(to, SUB), :] = fields[k][r * SUB : (r + 1) * SUB, cols(c)]
                block = rows + r * (SUB // per_block)
                two = [jnp.broadcast_to(fields[k][block + i : block + i + 1, cols(c)], (SUB, LANES)) for i in (0, 1)]
                conduct[c, pl.ds(PAD + to, SUB), :] = jnp.where(iota(0) < per_block, two[0], two[1])
    for r in range(count * rows // SUB):
        at = PAD + r * SUB
        here = [conduct[c, at : at + SUB, :] for c in range(tiles)]
        for c in range(tiles):
            left, right = beside(here, c, zero)
            above = conduct[c, at - 1 : at + SUB - 1, :]
            below = conduct[c, at + 1 : at + SUB + 1, :]
            own = weights[0, c, r * SUB : (r + 1) * SUB, :]
            w = [own * jnp.sqrt(here[c] * other) for other in (above, below, left, right)]
            weights[0, c, r * SUB : (r + 1) * SUB, :] = ((w[0] + w[1]) + w[2]) + w[3]
            for k in range(4):
                weights[k + 1, c, r * SUB : (r + 1) * SUB, :] = w[k]


def link_steps(state, weights, factor):
    _, tiles, padded, _ = state.shape

    def step(now):
        for r in range((padded - 2 * PAD) // SUB):
            at = PAD + r * SUB
            here = [state[now, c, at : at + SUB, :] for c in range(tiles)]
            for c in range(tiles):
                left, right = beside(here, c)
                above = state[now, c, at - 1 : at + SUB - 1, :]
                below = state[now, c, at + 1 : at + SUB + 1, :]
                w = [weights[k, c, r * SUB : (r + 1) * SUB, :] for k in range(5)]
                change = (w[1] * above + w[2] * below) + (w[3] * left + w[4] * right) - w[0] * here[c]
                state[1 - now, c, at : at + SUB, :] = here[c] + factor * change

    def one(i, now):
        step(now)
        return 1 - now

    return one


def scan_body(stage, final, refs):
    total, got, before, weights, steps = refs[:5]
    tiles, height, _ = total.shape
    size = 1 << stage
    mine, strip = lax.axis_index("tm"), lax.axis_index("space")
    upper = lax.rem(mine // size, 2) == 1
    first = (mine // (2 * size)) * (2 * size) + size
    if final:
        relaxed, out, state, errors, tmp = refs[5:]
        rows = 2 * relaxed.shape[0] // 4
    else:
        total_out, errors, state = refs[5:]
        rows = errors.shape[1]
    mine_rows = pl.multiple_of(strip * rows, SUB)
    zero = jnp.zeros((SUB, LANES), F32)
    for c in range(tiles):
        for b in (0, 1):
            state[b, c, 0:PAD, :] = zero
            state[b, c, PAD + height :, :] = zero

    def load(ref):
        for c in range(tiles):
            for r in range(height // SUB):
                state[0, c, PAD + r * SUB : PAD + (r + 1) * SUB, :] = ref[c, r * SUB : (r + 1) * SUB, :]

    @pl.when(upper)
    def _():
        load(got)

    @pl.when(jnp.logical_not(upper))
    def _():
        load(total)

    def keep(now):
        for c in range(tiles):
            piece = state[now, c, pl.ds(PAD + mine_rows, rows), :]
            errors[c, :, :] = piece if before is None else before[c, :, :] + piece

    def pass_on():
        for c in range(tiles):
            if before is None:
                errors[c, :, :] = jnp.zeros((rows, LANES), F32)
            else:
                errors[c, :, :] = before[c, :, :]

    pass_on()

    def turn(i, now):
        @pl.when(jnp.logical_and(upper, first + i == mine))
        def _():
            keep(now)

        factor = steps[first + i].astype(F32) * (1.0 / (4.0 * CSUB))
        return lax.fori_loop(0, CSUB, link_steps(state, weights, factor), now)

    if final:
        turns = jnp.where(upper, mine - first, 0)
        now = lax.fori_loop(0, turns, turn, jnp.int32(0))

        @pl.when(upper)
        def _():
            keep(now)

        pairs = double()
        for c in range(tiles):
            wide = dot(errors[c, :, :], pairs)
            for k in (0, 1):
                part = wide[:, k * LANES : (k + 1) * LANES]
                tmp[2 * c + k, pl.ds(0, rows, stride=2), :] = part
                tmp[2 * c + k, pl.ds(1, rows, stride=2), :] = part
        for c in range(2 * tiles):
            out[:, cols(c)] = relaxed[:, cols(c)] + tmp[c, :, :]
    else:
        now = lax.fori_loop(0, size, turn, jnp.int32(0))

        def close(ref):
            for c in range(tiles):
                for r in range(height // SUB):
                    at = slice(r * SUB, (r + 1) * SUB)
                    total_out[c, at, :] = ref[c, at, :] + state[now, c, pl.ds(PAD + r * SUB, SUB), :]

        @pl.when(upper)
        def _():
            close(total)

        @pl.when(jnp.logical_not(upper))
        def _():
            close(got)


def shards(point_states, initial_state, node_rate, source_map, waveform, cond_table, class_map, interval_steps):
    assert point_states.shape[0] == 1
    intervals, strips = lax.axis_size("tm"), lax.axis_size("space")
    assert intervals & (intervals - 1) == 0 and strips & (strips - 1) == 0
    point = point_states[0]
    rows, width = point.shape
    tiles, ctiles, crows, blocks = width // LANES, width // LANES // 2, rows // 2, rows // BLK_R
    height, cheight = rows + 2 * HALO, crows * strips
    packed = -(-(3 * STEP_MOST + HT) // SUB) * SUB
    fields_rows = -(-(crows + blocks) // SUB) * SUB
    both = ("tm", "space")

    def side(s, which):
        other = s ^ 1 if which == "a" else (s + 1 if s % 2 else s - 1)
        return other if 0 <= other < strips else None

    def exchange(value, ahead, move):
        pairs = []
        for j in range(intervals):
            for s in range(strips):
                to = move(s)
                if to is not None:
                    pairs.append((j * strips + s, ((j + ahead) % intervals) * strips + to))
        return lax.ppermute(value, both, pairs)

    pay_a, pay_b, field = call(
        pack_body, [VM, VM, VM, SM, SM],
        (f32(packed, width), f32(packed, width), f32(fields_rows, width // 2)),
        [pltpu.VMEM((tiles, rows, LANES), F32)], 1 << 20,
    )(point, node_rate, source_map, cond_table, class_map)
    got_a = exchange(pay_a, 0, lambda s: side(s, "a"))
    got_b = exchange(pay_b, 0, lambda s: side(s, "b"))
    fields = [field] + [exchange(field, 0, lambda s, k=k: s ^ k) for k in range(1, strips)]

    passed, edge_a, edge_b, weights = call(
        first_body, [VM] * 6 + [SM] * 4,
        (f32(rows, width), f32(HALO, width), f32(HALO, width), f32(5, tiles, height, LANES)),
        [
            pltpu.VMEM((2, tiles, height + 2 * PAD, LANES), F32),
            pltpu.VMEM((tiles, height, LANES), F32),
            pltpu.VMEM((tiles, height, LANES), F32),
            pltpu.VMEM((tiles, height + 2 * PAD, LANES), F32),
        ],
        1 << 24,
    )(point, node_rate, source_map, got_a, got_b, initial_state, cond_table, class_map, interval_steps, waveform)
    relaxed = exchange(passed, 1, lambda s: s)
    edge_a = exchange(edge_a, 1, lambda s: side(s, "a"))
    edge_b = exchange(edge_b, 1, lambda s: side(s, "b"))

    change = call(
        second_body, [VM] * 7 + [SM], f32(crows, width // 2),
        [pltpu.VMEM((2, tiles, height + 2 * PAD, LANES), F32), pltpu.VMEM((tiles, height, LANES), F32)],
        1 << 24,
    )(relaxed, edge_a, edge_b, point, got_a, got_b, weights, interval_steps)
    changes = [change] + [exchange(change, 0, lambda s, k=k: s ^ k) for k in range(1, strips)]

    def assemble(*refs):
        assemble_body(refs[:strips], refs[strips : 2 * strips], *refs[2 * strips :])

    total, coarse_weights = call(
        assemble, [VM] * (2 * strips), (f32(ctiles, cheight, LANES), f32(5, ctiles, cheight, LANES)),
        [pltpu.VMEM((ctiles, cheight + 2 * PAD, LANES), F32)], 1 << 20,
    )(*changes, *fields)

    errors = None
    stages = intervals.bit_length() - 1
    for stage in range(stages):
        got = lax.ppermute(total, "tm", [(j, j ^ (1 << stage)) for j in range(intervals)])
        final = stage == stages - 1
        some = errors is not None

        def body(*refs, stage=stage, final=final, some=some):
            refs = refs if some else (*refs[:2], None, *refs[2:])
            scan_body(stage, final, refs)

        state = pltpu.VMEM((2, ctiles, cheight + 2 * PAD, LANES), F32)
        lead = [total, got] + ([errors] if some else []) + [coarse_weights, interval_steps]
        specs = [VM] * (len(lead) - 1) + [SM]
        if final:
            out = call(
                body, specs + [VM], f32(rows, width),
                [state, pltpu.VMEM((ctiles, crows, LANES), F32), pltpu.VMEM((tiles, rows, LANES), F32)], 1 << 23,
            )(*lead, relaxed)
        else:
            total, errors = call(
                body, specs, (f32(ctiles, cheight, LANES), f32(ctiles, crows, LANES)), [state], 1 << 23
            )(*lead)
    return out[None]


def solution(mesh):
    placed = (
        P("tm", "space", None),
        P("space", None),
        P("space", None),
        P("space", None),
        P(),
        P(),
        P("space", None),
        P(),
    )
    return jax.shard_map(shards, mesh=mesh, in_specs=placed, out_specs=P("tm", "space", None), check_vma=False)
```

```python
import functools

import jax
import jax.numpy as jnp
from jax import lax
from jax.experimental import pallas as pl
from jax.experimental.pallas import tpu as pltpu
from jax.sharding import PartitionSpec as P

STEP_MOST = 20
CSUB = 5
BLK_R = 8
BLK_C = 128
SUB = 8
LANES = 128
MAIN = STEP_MOST // SUB * SUB
REST = STEP_MOST - MAIN
HALO = -(-STEP_MOST // SUB) * SUB
HT = HALO // SUB
PAD = SUB
VM = pl.BlockSpec(memory_space=pltpu.VMEM)
SM = pl.BlockSpec(memory_space=pltpu.SMEM)
F32 = jnp.float32


def f32(*shape):
    return jax.ShapeDtypeStruct(shape, F32)


def call(body, ins, outs, scratch, flops):
    return pl.pallas_call(
        body,
        out_shape=outs,
        in_specs=ins,
        out_specs=jax.tree.map(lambda _: VM, outs),
        scratch_shapes=scratch,
        cost_estimate=pl.CostEstimate(flops=flops, bytes_accessed=1 << 20, transcendentals=0),
    )


def iota(axis, shape=(SUB, LANES)):
    return lax.broadcasted_iota(jnp.int32, shape, axis)


def cols(c):
    return slice(c * LANES, (c + 1) * LANES)


def beside(tiles, c, left_edge=None):
    lane = iota(1)
    before = pltpu.roll(tiles[c], 1, 1)
    after = pltpu.roll(tiles[c], LANES - 1, 1)
    if c > 0:
        before = jnp.where(lane == 0, pltpu.roll(tiles[c - 1], 1, 1), before)
    elif left_edge is not None:
        before = jnp.where(lane == 0, left_edge, before)
    if c + 1 < len(tiles):
        after = jnp.where(lane == LANES - 1, pltpu.roll(tiles[c + 1], LANES - 1, 1), after)
    elif left_edge is not None:
        after = jnp.where(lane == LANES - 1, left_edge, after)
    return before, after


def halve():
    wide, narrow = iota(0, (2 * LANES, LANES)), iota(1, (2 * LANES, LANES))
    return jnp.where(wide // 2 == narrow, 1.0, 0.0).astype(F32)


def double():
    narrow, wide = iota(0, (LANES, 2 * LANES)), iota(1, (LANES, 2 * LANES))
    return jnp.where(wide // 2 == narrow, 1.0, 0.0).astype(F32)


def dot(a, b):
    return jnp.dot(a, b, precision=lax.Precision.HIGHEST, preferred_element_type=F32)


def row_pairs(ref, index, first, rows):
    top = ref[(*index, pl.ds(first, rows, stride=2), slice(None))]
    return top + ref[(*index, pl.ds(first + 1, rows, stride=2), slice(None))]


def pack_body(point, rate, source, table, classes, pay_a, pay_b, coarse, tmp):
    rows, width = point.shape
    blocks, tiles = rows // BLK_R, width // LANES
    odd = lax.rem(lax.axis_index("space"), 2) == 1

    def fill(out, high):
        main = rows - MAIN if high else 0
        rest = rows - MAIN - REST if high else MAIN
        for i, ref in enumerate((point, rate, source)):
            out[i * MAIN : (i + 1) * MAIN, :] = ref[main : main + MAIN, :]
            at = 3 * MAIN + i * REST
            out[at : at + REST, :] = ref[rest : rest + REST, :]
        first = blocks - HT if high else 0
        for b in range(HT):
            for c in range(tiles):
                value = table[classes[first + b, c]]
                at = 3 * MAIN + 3 * REST + b
                out[at : at + 1, cols(c)] = jnp.full((1, LANES), value, F32)

    @pl.when(odd)
    def _():
        fill(pay_a, False)
        fill(pay_b, True)

    @pl.when(jnp.logical_not(odd))
    def _():
        fill(pay_a, True)
        fill(pay_b, False)

    for c in range(tiles):
        tmp[c, :, :] = rate[:, cols(c)]
    pairs = halve()
    for c in range(tiles // 2):
        wide = jnp.concatenate([row_pairs(tmp, (2 * c + k,), 0, rows // 2) for k in (0, 1)], axis=1)
        coarse[: rows // 2, cols(c)] = 0.25 * dot(wide, pairs)
        for b in range(blocks):
            halves = [jnp.full((1, LANES), table[classes[b, 2 * c + k]], F32) for k in (0, 1)]
            at = rows // 2 + b
            coarse[at : at + 1, cols(c)] = jnp.where(iota(1, (1, LANES)) < LANES // 2, halves[0], halves[1])


def sweep(state, spare, weights, force, count, tiles, strip_tiles, wave):
    def step(source, target, t, reach):
        amount = None if wave is None else wave(t)
        for r in range(HT - reach, HT + strip_tiles + reach):
            at = PAD + r * SUB
            here = [source[c, at : at + SUB, :] for c in range(tiles)]
            for c in range(tiles):
                left, right = beside(here, c)
                above = source[c, at - 1 : at + SUB - 1, :]
                below = source[c, at + 1 : at + SUB + 1, :]
                w = [weights[k, c, r * SUB : (r + 1) * SUB, :] for k in range(5)]
                new = (w[0] * here[c] + w[1] * above) + (w[2] * below + w[3] * left) + w[4] * right
                if amount is not None:
                    new = new + amount * force[c, r * SUB : (r + 1) * SUB, :]
                target[c, at : at + SUB, :] = new

    def pair(p, _, reach):
        step(state, spare, 2 * p, reach)
        step(spare, state, 2 * p + 1, reach)

    begin = 0
    for reach in range(HT, 0, -1):
        end = jnp.maximum(count - SUB * (reach - 1), 0) // 2
        lax.fori_loop(begin, end, functools.partial(pair, reach=reach), None)
        begin = end

    @pl.when(lax.rem(count, 2) == 1)
    def _():
        step(state, spare, count - 1, 0)
        for c in range(tiles):
            for r in range(strip_tiles):
                at = PAD + HALO + r * SUB
                state[c, at : at + SUB, :] = spare[c, at : at + SUB, :]


def with_halos(odd, got_a, got_b, place):
    @pl.when(odd)
    def _():
        place(got_a, True)
        place(got_b, False)

    @pl.when(jnp.logical_not(odd))
    def _():
        place(got_b, True)
        place(got_a, False)


def unpack(out, tiles, rows, payload, above, which, at=0):
    for c in range(tiles):
        if above:
            main, rest = at + HALO - MAIN, at + HALO - MAIN - REST
        else:
            main, rest = at + HALO + rows, at + HALO + rows + MAIN
        first = 3 * MAIN + which * REST
        out[c, main : main + MAIN, :] = payload[which * MAIN : (which + 1) * MAIN, cols(c)]
        out[c, rest : rest + REST, :] = payload[first : first + REST, cols(c)]


def first_body(
    point, rate, source, got_a, got_b, initial, table, classes, steps, waveform,
    relaxed, edge_a, edge_b, weights, state, spare, force, rates, conduct,
):
    rows, width = point.shape
    tiles, strip_tiles, blocks = width // LANES, rows // SUB, rows // BLK_R
    mine, strip = lax.axis_index("tm"), lax.axis_index("space")
    odd = lax.rem(strip, 2) == 1
    start = lax.fori_loop(0, mine, lambda i, total: total + steps[i], jnp.int32(0))
    count = steps[mine]

    for c in range(tiles):
        for r in range(strip_tiles):
            at, to = slice(r * SUB, (r + 1) * SUB), slice(HALO + r * SUB, HALO + (r + 1) * SUB)
            state[c, PAD + HALO + r * SUB : PAD + HALO + (r + 1) * SUB, :] = point[at, cols(c)]
            rates[c, to, :] = rate[at, cols(c)]
            force[c, to, :] = source[at, cols(c)]
        for b in range(blocks):
            at = PAD + HALO + b * BLK_R
            conduct[c, at : at + BLK_R, :] = jnp.full((BLK_R, LANES), table[classes[b, c]], F32)
        zero = jnp.zeros((SUB, LANES), F32)
        conduct[c, 0:PAD, :] = zero
        conduct[c, PAD + 2 * HALO + rows :, :] = zero
        for at in (0, HALO + rows + HALO - SUB):
            rates[c, at : at + SUB, :] = zero
            force[c, at : at + SUB, :] = zero
            state[c, PAD + at : PAD + at + SUB, :] = zero

    def place(payload, above):
        unpack(state, tiles, rows, payload, above, 0, PAD)
        unpack(rates, tiles, rows, payload, above, 1)
        unpack(force, tiles, rows, payload, above, 2)
        for b in range(HT):
            at = PAD + b * BLK_R + (0 if above else HALO + rows)
            row = 3 * MAIN + 3 * REST + b
            for c in range(tiles):
                conduct[c, at : at + BLK_R, :] = jnp.broadcast_to(payload[row : row + 1, cols(c)], (BLK_R, LANES))

    with_halos(odd, got_a, got_b, place)

    zero = jnp.zeros((SUB, LANES), F32)
    for r in range(2 * HT + strip_tiles):
        at = PAD + r * SUB
        here = [conduct[c, at : at + SUB, :] for c in range(tiles)]
        for c in range(tiles):
            left, right = beside(here, c, zero)
            above = conduct[c, at - 1 : at + SUB - 1, :]
            below = conduct[c, at + 1 : at + SUB + 1, :]
            own = rates[c, r * SUB : (r + 1) * SUB, :]
            w = [own * jnp.sqrt(here[c] * other) for other in (above, below, left, right)]
            weights[0, c, r * SUB : (r + 1) * SUB, :] = 1.0 - (((w[0] + w[1]) + w[2]) + w[3])
            for k in range(4):
                weights[k + 1, c, r * SUB : (r + 1) * SUB, :] = w[k]

    sweep(state, spare, weights, force, count, tiles, strip_tiles, lambda t: waveform[start + t])

    def give(read):
        for c in range(tiles):
            for r in range(strip_tiles):
                relaxed[r * SUB : (r + 1) * SUB, cols(c)] = read(r, c)

        @pl.when(odd)
        def _():
            for c in range(tiles):
                for r in range(HT):
                    edge_a[r * SUB : (r + 1) * SUB, cols(c)] = read(r, c)
                    edge_b[r * SUB : (r + 1) * SUB, cols(c)] = read(strip_tiles - HT + r, c)

        @pl.when(jnp.logical_not(odd))
        def _():
            for c in range(tiles):
                for r in range(HT):
                    edge_b[r * SUB : (r + 1) * SUB, cols(c)] = read(r, c)
                    edge_a[r * SUB : (r + 1) * SUB, cols(c)] = read(strip_tiles - HT + r, c)

    last = mine == lax.axis_size("tm") - 1

    @pl.when(last)
    def _():
        give(lambda r, c: initial[r * SUB : (r + 1) * SUB, cols(c)])

    @pl.when(jnp.logical_not(last))
    def _():
        give(lambda r, c: state[c, PAD + HALO + r * SUB : PAD + HALO + (r + 1) * SUB, :])


def second_body(relaxed, edge_a, edge_b, point, got_a, got_b, weights, steps, coarse, state, spare, tmp):
    rows, width = point.shape
    tiles, strip_tiles = width // LANES, rows // SUB
    mine, strip = lax.axis_index("tm"), lax.axis_index("space")
    odd = lax.rem(strip, 2) == 1
    count = steps[mine]
    for c in range(tiles):
        for r in range(strip_tiles):
            at = slice(r * SUB, (r + 1) * SUB)
            to = PAD + HALO + r * SUB
            state[c, to : to + SUB, :] = relaxed[at, cols(c)] - point[at, cols(c)]
        for at in (0, HALO + rows + HALO - SUB):
            tmp[c, at : at + SUB, :] = jnp.zeros((SUB, LANES), F32)

    def place(pair, above):
        edge, payload = pair
        unpack(tmp, tiles, rows, payload, above, 0)
        base = 0 if above else HALO + rows
        for c in range(tiles):
            for r in range(HT):
                at = base + r * SUB
                state[c, PAD + at : PAD + at + SUB, :] = edge[r * SUB : (r + 1) * SUB, cols(c)] - tmp[c, at : at + SUB, :]

    with_halos(odd, (edge_a, got_a), (edge_b, got_b), place)
    sweep(state, spare, weights, None, count, tiles, strip_tiles, None)
    pairs = halve()
    for c in range(tiles // 2):
        wide = [row_pairs(state, (2 * c + k,), PAD + HALO, rows // 2) for k in (0, 1)]
        coarse[:, cols(c)] = 0.25 * dot(jnp.concatenate(wide, axis=1), pairs)


def assemble_body(strips, fields, total, weights, conduct):
    count = len(strips)
    rows, width = strips[0].shape
    tiles = width // LANES
    mine = lax.axis_index("space")
    per_block = BLK_R // 2
    zero = jnp.zeros((SUB, LANES), F32)
    for c in range(tiles):
        conduct[c, 0:PAD, :] = zero
        conduct[c, PAD + count * rows :, :] = zero
    for k in range(count):
        base = (mine ^ k) * rows
        for c in range(tiles):
            for r in range(rows // SUB):
                to = pl.multiple_of(base + r * SUB, SUB)
                total[c, pl.ds(to, SUB), :] = strips[k][r * SUB : (r + 1) * SUB, cols(c)]
                weights[0, c, pl.ds(to, SUB), :] = fields[k][r * SUB : (r + 1) * SUB, cols(c)]
                block = rows + r * (SUB // per_block)
                two = [jnp.broadcast_to(fields[k][block + i : block + i + 1, cols(c)], (SUB, LANES)) for i in (0, 1)]
                conduct[c, pl.ds(PAD + to, SUB), :] = jnp.where(iota(0) < per_block, two[0], two[1])
    for r in range(count * rows // SUB):
        at = PAD + r * SUB
        here = [conduct[c, at : at + SUB, :] for c in range(tiles)]
        for c in range(tiles):
            left, right = beside(here, c, zero)
            above = conduct[c, at - 1 : at + SUB - 1, :]
            below = conduct[c, at + 1 : at + SUB + 1, :]
            own = weights[0, c, r * SUB : (r + 1) * SUB, :]
            w = [own * jnp.sqrt(here[c] * other) for other in (above, below, left, right)]
            weights[0, c, r * SUB : (r + 1) * SUB, :] = ((w[0] + w[1]) + w[2]) + w[3]
            for k in range(4):
                weights[k + 1, c, r * SUB : (r + 1) * SUB, :] = w[k]


def link(buffers, weights, factor):
    state, one, two = buffers
    tiles, padded, _ = state.shape

    def step(source, target):
        for r in range((padded - 2 * PAD) // SUB):
            at = PAD + r * SUB
            here = [source[c, at : at + SUB, :] for c in range(tiles)]
            for c in range(tiles):
                left, right = beside(here, c)
                above = source[c, at - 1 : at + SUB - 1, :]
                below = source[c, at + 1 : at + SUB + 1, :]
                w = [weights[k, c, r * SUB : (r + 1) * SUB, :] for k in range(5)]
                change = (w[1] * above + w[2] * below) + (w[3] * left + w[4] * right) - w[0] * here[c]
                target[c, at : at + SUB, :] = here[c] + factor * change

    source = state
    for k in range(CSUB):
        target = state if k == CSUB - 1 else (two if source is one else one)
        step(source, target)
        source = target


def scan_body(stage, final, refs):
    total, got, before, weights, steps = refs[:5]
    tiles, height, _ = total.shape
    size = 1 << stage
    mine, strip = lax.axis_index("tm"), lax.axis_index("space")
    upper = lax.rem(mine // size, 2) == 1
    first = (mine // (2 * size)) * (2 * size) + size
    if final:
        relaxed, out, *buffers, errors, tmp = refs[5:]
        rows = 2 * relaxed.shape[0] // 4
    else:
        total_out, errors, *buffers = refs[5:]
        rows = errors.shape[1]
    mine_rows = pl.multiple_of(strip * rows, SUB)
    zero = jnp.zeros((SUB, LANES), F32)
    state = buffers[0]
    for c in range(tiles):
        for buffer in buffers:
            buffer[c, 0:PAD, :] = zero
            buffer[c, PAD + height :, :] = zero

    def load(ref):
        for c in range(tiles):
            for r in range(height // SUB):
                state[c, PAD + r * SUB : PAD + (r + 1) * SUB, :] = ref[c, r * SUB : (r + 1) * SUB, :]

    @pl.when(upper)
    def _():
        load(got)

    @pl.when(jnp.logical_not(upper))
    def _():
        load(total)

    def keep():
        for c in range(tiles):
            piece = state[c, pl.ds(PAD + mine_rows, rows), :]
            errors[c, :, :] = piece if before is None else before[c, :, :] + piece

    def pass_on():
        for c in range(tiles):
            if before is None:
                errors[c, :, :] = jnp.zeros((rows, LANES), F32)
            else:
                errors[c, :, :] = before[c, :, :]

    pass_on()

    def turn(i, _):
        @pl.when(jnp.logical_and(upper, first + i == mine))
        def _():
            keep()

        link(buffers, weights, steps[first + i].astype(F32) * (1.0 / (4.0 * CSUB)))

    if final:
        turns = jnp.where(upper, mine - first, 0)
        lax.fori_loop(0, turns, turn, None)

        @pl.when(upper)
        def _():
            keep()

        pairs = double()
        for c in range(tiles):
            wide = dot(errors[c, :, :], pairs)
            for k in (0, 1):
                part = wide[:, k * LANES : (k + 1) * LANES]
                tmp[2 * c + k, pl.ds(0, rows, stride=2), :] = part
                tmp[2 * c + k, pl.ds(1, rows, stride=2), :] = part
        for c in range(2 * tiles):
            out[:, cols(c)] = relaxed[:, cols(c)] + tmp[c, :, :]
    else:
        lax.fori_loop(0, size, turn, None)

        def close(ref):
            for c in range(tiles):
                for r in range(height // SUB):
                    at = slice(r * SUB, (r + 1) * SUB)
                    total_out[c, at, :] = ref[c, at, :] + state[c, PAD + r * SUB : PAD + (r + 1) * SUB, :]

        @pl.when(upper)
        def _():
            close(total)

        @pl.when(jnp.logical_not(upper))
        def _():
            close(got)


def shards(point_states, initial_state, node_rate, source_map, waveform, cond_table, class_map, interval_steps):
    assert point_states.shape[0] == 1
    intervals, strips = lax.axis_size("tm"), lax.axis_size("space")
    assert intervals & (intervals - 1) == 0 and strips & (strips - 1) == 0
    point = point_states[0]
    rows, width = point.shape
    tiles, ctiles, crows, blocks = width // LANES, width // LANES // 2, rows // 2, rows // BLK_R
    height, cheight = rows + 2 * HALO, crows * strips
    packed = -(-(3 * STEP_MOST + HT) // SUB) * SUB
    fields_rows = -(-(crows + blocks) // SUB) * SUB
    both = ("tm", "space")

    def side(s, which):
        other = s ^ 1 if which == "a" else (s + 1 if s % 2 else s - 1)
        return other if 0 <= other < strips else None

    def exchange(value, ahead, move):
        pairs = []
        for j in range(intervals):
            for s in range(strips):
                to = move(s)
                if to is not None:
                    pairs.append((j * strips + s, ((j + ahead) % intervals) * strips + to))
        return lax.ppermute(value, both, pairs)

    pay_a, pay_b, field = call(
        pack_body, [VM, VM, VM, SM, SM],
        (f32(packed, width), f32(packed, width), f32(fields_rows, width // 2)),
        [pltpu.VMEM((tiles, rows, LANES), F32)], 1 << 20,
    )(point, node_rate, source_map, cond_table, class_map)
    got_a = exchange(pay_a, 0, lambda s: side(s, "a"))
    got_b = exchange(pay_b, 0, lambda s: side(s, "b"))
    fields = [field] + [exchange(field, 0, lambda s, k=k: s ^ k) for k in range(1, strips)]

    passed, edge_a, edge_b, weights = call(
        first_body, [VM] * 6 + [SM] * 4,
        (f32(rows, width), f32(HALO, width), f32(HALO, width), f32(5, tiles, height, LANES)),
        [
            pltpu.VMEM((tiles, height + 2 * PAD, LANES), F32),
            pltpu.VMEM((tiles, height + 2 * PAD, LANES), F32),
            pltpu.VMEM((tiles, height, LANES), F32),
            pltpu.VMEM((tiles, height, LANES), F32),
            pltpu.VMEM((tiles, height + 2 * PAD, LANES), F32),
        ],
        1 << 24,
    )(point, node_rate, source_map, got_a, got_b, initial_state, cond_table, class_map, interval_steps, waveform)
    relaxed = exchange(passed, 1, lambda s: s)
    edge_a = exchange(edge_a, 1, lambda s: side(s, "a"))
    edge_b = exchange(edge_b, 1, lambda s: side(s, "b"))

    change = call(
        second_body, [VM] * 7 + [SM], f32(crows, width // 2),
        [pltpu.VMEM((tiles, height + 2 * PAD, LANES), F32)] * 2 + [pltpu.VMEM((tiles, height, LANES), F32)],
        1 << 24,
    )(relaxed, edge_a, edge_b, point, got_a, got_b, weights, interval_steps)
    changes = [change] + [exchange(change, 0, lambda s, k=k: s ^ k) for k in range(1, strips)]

    def assemble(*refs):
        assemble_body(refs[:strips], refs[strips : 2 * strips], *refs[2 * strips :])

    total, coarse_weights = call(
        assemble, [VM] * (2 * strips), (f32(ctiles, cheight, LANES), f32(5, ctiles, cheight, LANES)),
        [pltpu.VMEM((ctiles, cheight + 2 * PAD, LANES), F32)], 1 << 20,
    )(*changes, *fields)

    errors = None
    stages = intervals.bit_length() - 1
    for stage in range(stages):
        got = lax.ppermute(total, "tm", [(j, j ^ (1 << stage)) for j in range(intervals)])
        final = stage == stages - 1
        some = errors is not None

        def body(*refs, stage=stage, final=final, some=some):
            refs = refs if some else (*refs[:2], None, *refs[2:])
            scan_body(stage, final, refs)

        buffers = [pltpu.VMEM((ctiles, cheight + 2 * PAD, LANES), F32)] * 3
        lead = [total, got] + ([errors] if some else []) + [coarse_weights, interval_steps]
        specs = [VM] * (len(lead) - 1) + [SM]
        if final:
            out = call(
                body, specs + [VM], f32(rows, width),
                buffers + [pltpu.VMEM((ctiles, crows, LANES), F32), pltpu.VMEM((tiles, rows, LANES), F32)], 1 << 23,
            )(*lead, relaxed)
        else:
            total, errors = call(
                body, specs, (f32(ctiles, cheight, LANES), f32(ctiles, crows, LANES)), buffers, 1 << 23
            )(*lead)
    return out[None]


def solution(mesh):
    placed = (
        P("tm", "space", None),
        P("space", None),
        P("space", None),
        P("space", None),
        P(),
        P(),
        P("space", None),
        P(),
    )
    return jax.shard_map(shards, mesh=mesh, in_specs=placed, out_specs=P("tm", "space", None), check_vma=False)
```

```python
import functools

import jax
import jax.numpy as jnp
from jax import lax
from jax.experimental import pallas as pl
from jax.experimental.pallas import tpu as pltpu
from jax.sharding import PartitionSpec as P

STEP_MOST = 20
CSUB = 5
BLK_R = 8
BLK_C = 128
SUB = 8
LANES = 128
MAIN = STEP_MOST // SUB * SUB
REST = STEP_MOST - MAIN
HALO = -(-STEP_MOST // SUB) * SUB
HT = HALO // SUB
PAD = SUB
VM = pl.BlockSpec(memory_space=pltpu.VMEM)
SM = pl.BlockSpec(memory_space=pltpu.SMEM)
F32 = jnp.float32
GRANT = 16 << 20


def f32(*shape):
    return jax.ShapeDtypeStruct(shape, F32)


def call(body, ins, outs, scratch, flops):
    return pl.pallas_call(
        body,
        out_shape=outs,
        in_specs=ins,
        out_specs=jax.tree.map(lambda _: VM, outs),
        scratch_shapes=scratch,
        compiler_params=pltpu.CompilerParams(vmem_limit_bytes=GRANT),
        cost_estimate=pl.CostEstimate(flops=flops, bytes_accessed=1 << 20, transcendentals=0),
    )


def iota(axis, shape=(SUB, LANES)):
    return lax.broadcasted_iota(jnp.int32, shape, axis)


def cols(c):
    return slice(c * LANES, (c + 1) * LANES)


def beside(tiles, c, left_edge=None):
    lane = iota(1)
    before = pltpu.roll(tiles[c], 1, 1)
    after = pltpu.roll(tiles[c], LANES - 1, 1)
    if c > 0:
        before = jnp.where(lane == 0, pltpu.roll(tiles[c - 1], 1, 1), before)
    elif left_edge is not None:
        before = jnp.where(lane == 0, left_edge, before)
    if c + 1 < len(tiles):
        after = jnp.where(lane == LANES - 1, pltpu.roll(tiles[c + 1], LANES - 1, 1), after)
    elif left_edge is not None:
        after = jnp.where(lane == LANES - 1, left_edge, after)
    return before, after


def halve():
    wide, narrow = iota(0, (2 * LANES, LANES)), iota(1, (2 * LANES, LANES))
    return jnp.where(wide // 2 == narrow, 1.0, 0.0).astype(F32)


def double():
    narrow, wide = iota(0, (LANES, 2 * LANES)), iota(1, (LANES, 2 * LANES))
    return jnp.where(wide // 2 == narrow, 1.0, 0.0).astype(F32)


def dot(a, b):
    return jnp.dot(a, b, precision=lax.Precision.HIGHEST, preferred_element_type=F32)


def row_pairs(ref, index, first, rows):
    top = ref[(*index, pl.ds(first, rows, stride=2), slice(None))]
    return top + ref[(*index, pl.ds(first + 1, rows, stride=2), slice(None))]


def pack_body(point, rate, source, table, classes, pay_a, pay_b, coarse, tmp):
    rows, width = point.shape
    blocks, tiles = rows // BLK_R, width // LANES
    odd = lax.rem(lax.axis_index("space"), 2) == 1

    def fill(out, high):
        main = rows - MAIN if high else 0
        rest = rows - MAIN - REST if high else MAIN
        for i, ref in enumerate((point, rate, source)):
            out[i * MAIN : (i + 1) * MAIN, :] = ref[main : main + MAIN, :]
            at = 3 * MAIN + i * REST
            out[at : at + REST, :] = ref[rest : rest + REST, :]
        first = blocks - HT if high else 0
        for b in range(HT):
            for c in range(tiles):
                value = table[classes[first + b, c]]
                at = 3 * MAIN + 3 * REST + b
                out[at : at + 1, cols(c)] = jnp.full((1, LANES), value, F32)

    @pl.when(odd)
    def _():
        fill(pay_a, False)
        fill(pay_b, True)

    @pl.when(jnp.logical_not(odd))
    def _():
        fill(pay_a, True)
        fill(pay_b, False)

    for c in range(tiles):
        tmp[c, :, :] = rate[:, cols(c)]
    pairs = halve()
    for c in range(tiles // 2):
        wide = jnp.concatenate([row_pairs(tmp, (2 * c + k,), 0, rows // 2) for k in (0, 1)], axis=1)
        coarse[: rows // 2, cols(c)] = 0.25 * dot(wide, pairs)
        for b in range(blocks):
            halves = [jnp.full((1, LANES), table[classes[b, 2 * c + k]], F32) for k in (0, 1)]
            at = rows // 2 + b
            coarse[at : at + 1, cols(c)] = jnp.where(iota(1, (1, LANES)) < LANES // 2, halves[0], halves[1])


def sweep(state, spare, weights, force, count, tiles, strip_tiles, wave):
    def step(source, target, t, reach):
        amount = None if wave is None else wave(t)
        for r in range(HT - reach, HT + strip_tiles + reach):
            at = PAD + r * SUB
            here = [source[c, at : at + SUB, :] for c in range(tiles)]
            for c in range(tiles):
                left, right = beside(here, c)
                above = source[c, at - 1 : at + SUB - 1, :]
                below = source[c, at + 1 : at + SUB + 1, :]
                w = [weights[k, c, r * SUB : (r + 1) * SUB, :] for k in range(5)]
                new = (w[0] * here[c] + w[1] * above) + (w[2] * below + w[3] * left) + w[4] * right
                if amount is not None:
                    new = new + amount * force[c, r * SUB : (r + 1) * SUB, :]
                target[c, at : at + SUB, :] = new

    def pair(p, _, reach):
        step(state, spare, 2 * p, reach)
        step(spare, state, 2 * p + 1, reach)

    begin = 0
    for reach in range(HT, 0, -1):
        end = jnp.maximum(count - SUB * (reach - 1), 0) // 2
        lax.fori_loop(begin, end, functools.partial(pair, reach=reach), None)
        begin = end

    @pl.when(lax.rem(count, 2) == 1)
    def _():
        step(state, spare, count - 1, 0)
        for c in range(tiles):
            for r in range(strip_tiles):
                at = PAD + HALO + r * SUB
                state[c, at : at + SUB, :] = spare[c, at : at + SUB, :]


def with_halos(odd, got_a, got_b, place):
    @pl.when(odd)
    def _():
        place(got_a, True)
        place(got_b, False)

    @pl.when(jnp.logical_not(odd))
    def _():
        place(got_b, True)
        place(got_a, False)


def unpack(out, tiles, rows, payload, above, which, at=0):
    for c in range(tiles):
        if above:
            main, rest = at + HALO - MAIN, at + HALO - MAIN - REST
        else:
            main, rest = at + HALO + rows, at + HALO + rows + MAIN
        first = 3 * MAIN + which * REST
        out[c, main : main + MAIN, :] = payload[which * MAIN : (which + 1) * MAIN, cols(c)]
        out[c, rest : rest + REST, :] = payload[first : first + REST, cols(c)]


def first_body(
    point, rate, source, got_a, got_b, initial, table, classes, steps, waveform,
    relaxed, edge_a, edge_b, weights, state, spare, force, rates, conduct,
):
    rows, width = point.shape
    tiles, strip_tiles, blocks = width // LANES, rows // SUB, rows // BLK_R
    mine, strip = lax.axis_index("tm"), lax.axis_index("space")
    odd = lax.rem(strip, 2) == 1
    start = lax.fori_loop(0, mine, lambda i, total: total + steps[i], jnp.int32(0))
    count = steps[mine]

    for c in range(tiles):
        for r in range(strip_tiles):
            at, to = slice(r * SUB, (r + 1) * SUB), slice(HALO + r * SUB, HALO + (r + 1) * SUB)
            state[c, PAD + HALO + r * SUB : PAD + HALO + (r + 1) * SUB, :] = point[at, cols(c)]
            rates[c, to, :] = rate[at, cols(c)]
            force[c, to, :] = source[at, cols(c)]
        for b in range(blocks):
            at = PAD + HALO + b * BLK_R
            conduct[c, at : at + BLK_R, :] = jnp.full((BLK_R, LANES), table[classes[b, c]], F32)
        zero = jnp.zeros((SUB, LANES), F32)
        conduct[c, 0:PAD, :] = zero
        conduct[c, PAD + 2 * HALO + rows :, :] = zero
        for at in (0, HALO + rows + HALO - SUB):
            rates[c, at : at + SUB, :] = zero
            force[c, at : at + SUB, :] = zero
            state[c, PAD + at : PAD + at + SUB, :] = zero

    def place(payload, above):
        unpack(state, tiles, rows, payload, above, 0, PAD)
        unpack(rates, tiles, rows, payload, above, 1)
        unpack(force, tiles, rows, payload, above, 2)
        for b in range(HT):
            at = PAD + b * BLK_R + (0 if above else HALO + rows)
            row = 3 * MAIN + 3 * REST + b
            for c in range(tiles):
                conduct[c, at : at + BLK_R, :] = jnp.broadcast_to(payload[row : row + 1, cols(c)], (BLK_R, LANES))

    with_halos(odd, got_a, got_b, place)

    zero = jnp.zeros((SUB, LANES), F32)
    for r in range(2 * HT + strip_tiles):
        at = PAD + r * SUB
        here = [conduct[c, at : at + SUB, :] for c in range(tiles)]
        for c in range(tiles):
            left, right = beside(here, c, zero)
            above = conduct[c, at - 1 : at + SUB - 1, :]
            below = conduct[c, at + 1 : at + SUB + 1, :]
            own = rates[c, r * SUB : (r + 1) * SUB, :]
            w = [own * jnp.sqrt(here[c] * other) for other in (above, below, left, right)]
            weights[0, c, r * SUB : (r + 1) * SUB, :] = 1.0 - (((w[0] + w[1]) + w[2]) + w[3])
            for k in range(4):
                weights[k + 1, c, r * SUB : (r + 1) * SUB, :] = w[k]

    sweep(state, spare, weights, force, count, tiles, strip_tiles, lambda t: waveform[start + t])

    def give(read):
        for c in range(tiles):
            for r in range(strip_tiles):
                relaxed[r * SUB : (r + 1) * SUB, cols(c)] = read(r, c)

        @pl.when(odd)
        def _():
            for c in range(tiles):
                for r in range(HT):
                    edge_a[r * SUB : (r + 1) * SUB, cols(c)] = read(r, c)
                    edge_b[r * SUB : (r + 1) * SUB, cols(c)] = read(strip_tiles - HT + r, c)

        @pl.when(jnp.logical_not(odd))
        def _():
            for c in range(tiles):
                for r in range(HT):
                    edge_b[r * SUB : (r + 1) * SUB, cols(c)] = read(r, c)
                    edge_a[r * SUB : (r + 1) * SUB, cols(c)] = read(strip_tiles - HT + r, c)

    last = mine == lax.axis_size("tm") - 1

    @pl.when(last)
    def _():
        give(lambda r, c: initial[r * SUB : (r + 1) * SUB, cols(c)])

    @pl.when(jnp.logical_not(last))
    def _():
        give(lambda r, c: state[c, PAD + HALO + r * SUB : PAD + HALO + (r + 1) * SUB, :])


def second_body(relaxed, edge_a, edge_b, point, got_a, got_b, weights, steps, coarse, state, spare, tmp):
    rows, width = point.shape
    tiles, strip_tiles = width // LANES, rows // SUB
    mine, strip = lax.axis_index("tm"), lax.axis_index("space")
    odd = lax.rem(strip, 2) == 1
    count = steps[mine]
    for c in range(tiles):
        for r in range(strip_tiles):
            at = slice(r * SUB, (r + 1) * SUB)
            to = PAD + HALO + r * SUB
            state[c, to : to + SUB, :] = relaxed[at, cols(c)] - point[at, cols(c)]
        for at in (0, HALO + rows + HALO - SUB):
            tmp[c, at : at + SUB, :] = jnp.zeros((SUB, LANES), F32)

    def place(pair, above):
        edge, payload = pair
        unpack(tmp, tiles, rows, payload, above, 0)
        base = 0 if above else HALO + rows
        for c in range(tiles):
            for r in range(HT):
                at = base + r * SUB
                state[c, PAD + at : PAD + at + SUB, :] = edge[r * SUB : (r + 1) * SUB, cols(c)] - tmp[c, at : at + SUB, :]

    with_halos(odd, (edge_a, got_a), (edge_b, got_b), place)
    sweep(state, spare, weights, None, count, tiles, strip_tiles, None)
    pairs = halve()
    for c in range(tiles // 2):
        wide = [row_pairs(state, (2 * c + k,), PAD + HALO, rows // 2) for k in (0, 1)]
        coarse[:, cols(c)] = 0.25 * dot(jnp.concatenate(wide, axis=1), pairs)


def assemble_body(strips, fields, total, weights, conduct):
    count = len(strips)
    rows, width = strips[0].shape
    tiles = width // LANES
    mine = lax.axis_index("space")
    per_block = BLK_R // 2
    zero = jnp.zeros((SUB, LANES), F32)
    for c in range(tiles):
        conduct[c, 0:PAD, :] = zero
        conduct[c, PAD + count * rows :, :] = zero
    for k in range(count):
        base = (mine ^ k) * rows
        for c in range(tiles):
            for r in range(rows // SUB):
                to = pl.multiple_of(base + r * SUB, SUB)
                total[c, pl.ds(to, SUB), :] = strips[k][r * SUB : (r + 1) * SUB, cols(c)]
                weights[0, c, pl.ds(to, SUB), :] = fields[k][r * SUB : (r + 1) * SUB, cols(c)]
                block = rows + r * (SUB // per_block)
                two = [jnp.broadcast_to(fields[k][block + i : block + i + 1, cols(c)], (SUB, LANES)) for i in (0, 1)]
                conduct[c, pl.ds(PAD + to, SUB), :] = jnp.where(iota(0) < per_block, two[0], two[1])
    for r in range(count * rows // SUB):
        at = PAD + r * SUB
        here = [conduct[c, at : at + SUB, :] for c in range(tiles)]
        for c in range(tiles):
            left, right = beside(here, c, zero)
            above = conduct[c, at - 1 : at + SUB - 1, :]
            below = conduct[c, at + 1 : at + SUB + 1, :]
            own = weights[0, c, r * SUB : (r + 1) * SUB, :]
            w = [own * jnp.sqrt(here[c] * other) for other in (above, below, left, right)]
            weights[0, c, r * SUB : (r + 1) * SUB, :] = ((w[0] + w[1]) + w[2]) + w[3]
            for k in range(4):
                weights[k + 1, c, r * SUB : (r + 1) * SUB, :] = w[k]


def link(buffers, weights, factor):
    state, one, two = buffers
    tiles, padded, _ = state.shape

    def step(source, target):
        for r in range((padded - 2 * PAD) // SUB):
            at = PAD + r * SUB
            here = [source[c, at : at + SUB, :] for c in range(tiles)]
            for c in range(tiles):
                left, right = beside(here, c)
                above = source[c, at - 1 : at + SUB - 1, :]
                below = source[c, at + 1 : at + SUB + 1, :]
                w = [weights[k, c, r * SUB : (r + 1) * SUB, :] for k in range(5)]
                change = (w[1] * above + w[2] * below) + (w[3] * left + w[4] * right) - w[0] * here[c]
                target[c, at : at + SUB, :] = here[c] + factor * change

    source = state
    for k in range(CSUB):
        target = state if k == CSUB - 1 else (two if source is one else one)
        step(source, target)
        source = target


def scan_body(stage, final, refs):
    total, got, before, weights, steps = refs[:5]
    tiles, height, _ = total.shape
    size = 1 << stage
    mine, strip = lax.axis_index("tm"), lax.axis_index("space")
    upper = lax.rem(mine // size, 2) == 1
    first = (mine // (2 * size)) * (2 * size) + size
    if final:
        relaxed, out, *buffers, errors, tmp = refs[5:]
        rows = 2 * relaxed.shape[0] // 4
    else:
        total_out, errors, *buffers = refs[5:]
        rows = errors.shape[1]
    mine_rows = pl.multiple_of(strip * rows, SUB)
    zero = jnp.zeros((SUB, LANES), F32)
    state = buffers[0]
    for c in range(tiles):
        for buffer in buffers:
            buffer[c, 0:PAD, :] = zero
            buffer[c, PAD + height :, :] = zero

    def load(ref):
        for c in range(tiles):
            for r in range(height // SUB):
                state[c, PAD + r * SUB : PAD + (r + 1) * SUB, :] = ref[c, r * SUB : (r + 1) * SUB, :]

    @pl.when(upper)
    def _():
        load(got)

    @pl.when(jnp.logical_not(upper))
    def _():
        load(total)

    def keep():
        for c in range(tiles):
            piece = state[c, pl.ds(PAD + mine_rows, rows), :]
            errors[c, :, :] = piece if before is None else before[c, :, :] + piece

    def pass_on():
        for c in range(tiles):
            if before is None:
                errors[c, :, :] = jnp.zeros((rows, LANES), F32)
            else:
                errors[c, :, :] = before[c, :, :]

    pass_on()

    def turn(i, _):
        @pl.when(jnp.logical_and(upper, first + i == mine))
        def _():
            keep()

        link(buffers, weights, steps[first + i].astype(F32) * (1.0 / (4.0 * CSUB)))

    if final:
        turns = jnp.where(upper, mine - first, 0)
        lax.fori_loop(0, turns, turn, None)

        @pl.when(upper)
        def _():
            keep()

        pairs = double()
        for c in range(tiles):
            wide = dot(errors[c, :, :], pairs)
            for k in (0, 1):
                part = wide[:, k * LANES : (k + 1) * LANES]
                tmp[2 * c + k, pl.ds(0, rows, stride=2), :] = part
                tmp[2 * c + k, pl.ds(1, rows, stride=2), :] = part
        for c in range(2 * tiles):
            out[:, cols(c)] = relaxed[:, cols(c)] + tmp[c, :, :]
    else:
        lax.fori_loop(0, size, turn, None)

        def close(ref):
            for c in range(tiles):
                for r in range(height // SUB):
                    at = slice(r * SUB, (r + 1) * SUB)
                    total_out[c, at, :] = ref[c, at, :] + state[c, PAD + r * SUB : PAD + (r + 1) * SUB, :]

        @pl.when(upper)
        def _():
            close(total)

        @pl.when(jnp.logical_not(upper))
        def _():
            close(got)


def shards(point_states, initial_state, node_rate, source_map, waveform, cond_table, class_map, interval_steps):
    assert point_states.shape[0] == 1
    intervals, strips = lax.axis_size("tm"), lax.axis_size("space")
    assert intervals & (intervals - 1) == 0 and strips & (strips - 1) == 0
    point = point_states[0]
    rows, width = point.shape
    tiles, ctiles, crows, blocks = width // LANES, width // LANES // 2, rows // 2, rows // BLK_R
    height, cheight = rows + 2 * HALO, crows * strips
    packed = -(-(3 * STEP_MOST + HT) // SUB) * SUB
    fields_rows = -(-(crows + blocks) // SUB) * SUB
    both = ("tm", "space")

    def side(s, which):
        other = s ^ 1 if which == "a" else (s + 1 if s % 2 else s - 1)
        return other if 0 <= other < strips else None

    def exchange(value, ahead, move):
        pairs = []
        for j in range(intervals):
            for s in range(strips):
                to = move(s)
                if to is not None:
                    pairs.append((j * strips + s, ((j + ahead) % intervals) * strips + to))
        return lax.ppermute(value, both, pairs)

    pay_a, pay_b, field = call(
        pack_body, [VM, VM, VM, SM, SM],
        (f32(packed, width), f32(packed, width), f32(fields_rows, width // 2)),
        [pltpu.VMEM((tiles, rows, LANES), F32)], 1 << 20,
    )(point, node_rate, source_map, cond_table, class_map)
    got_a = exchange(pay_a, 0, lambda s: side(s, "a"))
    got_b = exchange(pay_b, 0, lambda s: side(s, "b"))
    fields = [field] + [exchange(field, 0, lambda s, k=k: s ^ k) for k in range(1, strips)]

    passed, edge_a, edge_b, weights = call(
        first_body, [VM] * 6 + [SM] * 4,
        (f32(rows, width), f32(HALO, width), f32(HALO, width), f32(5, tiles, height, LANES)),
        [
            pltpu.VMEM((tiles, height + 2 * PAD, LANES), F32),
            pltpu.VMEM((tiles, height + 2 * PAD, LANES), F32),
            pltpu.VMEM((tiles, height, LANES), F32),
            pltpu.VMEM((tiles, height, LANES), F32),
            pltpu.VMEM((tiles, height + 2 * PAD, LANES), F32),
        ],
        1 << 24,
    )(point, node_rate, source_map, got_a, got_b, initial_state, cond_table, class_map, interval_steps, waveform)
    relaxed = exchange(passed, 1, lambda s: s)
    edge_a = exchange(edge_a, 1, lambda s: side(s, "a"))
    edge_b = exchange(edge_b, 1, lambda s: side(s, "b"))

    change = call(
        second_body, [VM] * 7 + [SM], f32(crows, width // 2),
        [pltpu.VMEM((tiles, height + 2 * PAD, LANES), F32)] * 2 + [pltpu.VMEM((tiles, height, LANES), F32)],
        1 << 24,
    )(relaxed, edge_a, edge_b, point, got_a, got_b, weights, interval_steps)
    changes = [change] + [exchange(change, 0, lambda s, k=k: s ^ k) for k in range(1, strips)]

    def assemble(*refs):
        assemble_body(refs[:strips], refs[strips : 2 * strips], *refs[2 * strips :])

    total, coarse_weights = call(
        assemble, [VM] * (2 * strips), (f32(ctiles, cheight, LANES), f32(5, ctiles, cheight, LANES)),
        [pltpu.VMEM((ctiles, cheight + 2 * PAD, LANES), F32)], 1 << 20,
    )(*changes, *fields)

    errors = None
    stages = intervals.bit_length() - 1
    for stage in range(stages):
        got = lax.ppermute(total, "tm", [(j, j ^ (1 << stage)) for j in range(intervals)])
        final = stage == stages - 1
        some = errors is not None

        def body(*refs, stage=stage, final=final, some=some):
            refs = refs if some else (*refs[:2], None, *refs[2:])
            scan_body(stage, final, refs)

        buffers = [pltpu.VMEM((ctiles, cheight + 2 * PAD, LANES), F32)] * 3
        lead = [total, got] + ([errors] if some else []) + [coarse_weights, interval_steps]
        specs = [VM] * (len(lead) - 1) + [SM]
        if final:
            out = call(
                body, specs + [VM], f32(rows, width),
                buffers + [pltpu.VMEM((ctiles, crows, LANES), F32), pltpu.VMEM((tiles, rows, LANES), F32)], 1 << 23,
            )(*lead, relaxed)
        else:
            total, errors = call(
                body, specs, (f32(ctiles, cheight, LANES), f32(ctiles, crows, LANES)), buffers, 1 << 23
            )(*lead)
    return out[None]


def solution(mesh):
    placed = (
        P("tm", "space", None),
        P("space", None),
        P("space", None),
        P("space", None),
        P(),
        P(),
        P("space", None),
        P(),
    )
    return jax.shard_map(shards, mesh=mesh, in_specs=placed, out_specs=P("tm", "space", None), check_vma=False)
```

```python
import functools

import jax
import jax.numpy as jnp
from jax import lax
from jax.experimental import pallas as pl
from jax.experimental.pallas import tpu as pltpu
from jax.sharding import PartitionSpec as P


STEP_MOST = 20
CSUB = 5
BLK_R = 8
SUB = 8
LANES = 128
MAIN = STEP_MOST // SUB * SUB
REST = STEP_MOST - MAIN
HALO = -(-STEP_MOST // SUB) * SUB
HT = HALO // SUB
PAD = SUB
VM = pl.BlockSpec(memory_space=pltpu.VMEM)
SM = pl.BlockSpec(memory_space=pltpu.SMEM)
FAR = pl.BlockSpec(memory_space=pltpu.HBM)
F32 = jnp.float32
GRANT = 16 << 20


def f32(*shape):
    return jax.ShapeDtypeStruct(shape, F32)


def call(body, ins, outs, scratch, flops):
    return pl.pallas_call(
        body,
        out_shape=outs,
        in_specs=ins,
        out_specs=jax.tree.map(lambda _: VM, outs),
        scratch_shapes=scratch,
        compiler_params=pltpu.CompilerParams(vmem_limit_bytes=GRANT),
        cost_estimate=pl.CostEstimate(flops=flops, bytes_accessed=1 << 20, transcendentals=0),
    )


def far(value):
    return pltpu.with_memory_space_constraint(value, pltpu.HBM)


def iota(axis, shape=(SUB, LANES)):
    return lax.broadcasted_iota(jnp.int32, shape, axis)


def cols(c):
    return slice(c * LANES, (c + 1) * LANES)


def beside(tiles, c, left_edge=None):
    lane = iota(1)
    before = pltpu.roll(tiles[c], 1, 1)
    after = pltpu.roll(tiles[c], LANES - 1, 1)
    if c > 0:
        before = jnp.where(lane == 0, pltpu.roll(tiles[c - 1], 1, 1), before)
    elif left_edge is not None:
        before = jnp.where(lane == 0, left_edge, before)
    if c + 1 < len(tiles):
        after = jnp.where(lane == LANES - 1, pltpu.roll(tiles[c + 1], LANES - 1, 1), after)
    elif left_edge is not None:
        after = jnp.where(lane == LANES - 1, left_edge, after)
    return before, after


def halve():
    wide, narrow = iota(0, (2 * LANES, LANES)), iota(1, (2 * LANES, LANES))
    return jnp.where(wide // 2 == narrow, 1.0, 0.0).astype(F32)


def double():
    narrow, wide = iota(0, (LANES, 2 * LANES)), iota(1, (LANES, 2 * LANES))
    return jnp.where(wide // 2 == narrow, 1.0, 0.0).astype(F32)


def dot(a, b):
    return jnp.dot(a, b, precision=lax.Precision.HIGHEST, preferred_element_type=F32)


def row_pairs(ref, index, first, rows):
    top = ref[(*index, pl.ds(first, rows, stride=2), slice(None))]
    return top + ref[(*index, pl.ds(first + 1, rows, stride=2), slice(None))]


def fetch(pairs, sems):
    copies = [pltpu.make_async_copy(source, target, sems.at[i]) for i, (source, target) in enumerate(pairs)]
    for copy in copies:
        copy.start()
    return copies


def pack_body(
    point_far, rate_far, source_far, initial_far, table_far, classes_far,
    pay_a, pay_b, coarse, blocks_out, point, rate, source, initial, table, classes, tmp, sems,
):
    copies = fetch(
        (
            (table_far, table), (classes_far, classes), (rate_far, rate),
            (point_far, point), (source_far, source), (initial_far, initial),
        ), sems,
    )
    rows, width = point.shape
    blocks, tiles = rows // BLK_R, width // LANES
    odd = lax.rem(lax.axis_index("space"), 2) == 1
    copies[0].wait()
    copies[1].wait()
    for b in range(blocks):
        for c in range(tiles):
            blocks_out[b : b + 1, cols(c)] = jnp.full((1, LANES), table[classes[b, c]], F32)
    for copy in copies[2:5]:
        copy.wait()

    def fill(out, high):
        main = rows - MAIN if high else 0
        rest = rows - MAIN - REST if high else MAIN
        for i, ref in enumerate((point, rate, source)):
            out[i * MAIN : (i + 1) * MAIN, :] = ref[main : main + MAIN, :]
            at = 3 * MAIN + i * REST
            out[at : at + REST, :] = ref[rest : rest + REST, :]
        first = blocks - HT if high else 0
        at = 3 * MAIN + 3 * REST
        out[at : at + HT, :] = blocks_out[first : first + HT, :]

    @pl.when(odd)
    def _():
        fill(pay_a, False)
        fill(pay_b, True)

    @pl.when(jnp.logical_not(odd))
    def _():
        fill(pay_a, True)
        fill(pay_b, False)

    for c in range(tiles):
        tmp[c, :, :] = rate[:, cols(c)]
    pairs = halve()
    for c in range(tiles // 2):
        wide = jnp.concatenate([row_pairs(tmp, (2 * c + k,), 0, rows // 2) for k in (0, 1)], axis=1)
        coarse[: rows // 2, cols(c)] = 0.25 * dot(wide, pairs)
        halves = [blocks_out[0:blocks, cols(2 * c + k)] for k in (0, 1)]
        coarse[rows // 2 : rows // 2 + blocks, cols(c)] = jnp.where(
            iota(1, (blocks, LANES)) < LANES // 2, halves[0], halves[1]
        )
    copies[5].wait()


def sweep(state, spare, weights, force, count, tiles, strip_tiles, wave):
    def step(source, target, t, reach):
        amount = None if wave is None else wave(t)
        for r in range(HT - reach, HT + strip_tiles + reach):
            at = PAD + r * SUB
            here = [source[c, at : at + SUB, :] for c in range(tiles)]
            for c in range(tiles):
                left, right = beside(here, c)
                above = source[c, at - 1 : at + SUB - 1, :]
                below = source[c, at + 1 : at + SUB + 1, :]
                w = [weights[k, c, r * SUB : (r + 1) * SUB, :] for k in range(5)]
                new = (w[0] * here[c] + w[1] * above) + (w[2] * below + w[3] * left) + w[4] * right
                if amount is not None:
                    new = new + amount * force[c, r * SUB : (r + 1) * SUB, :]
                target[c, at : at + SUB, :] = new

    def pair(p, _, reach):
        step(state, spare, 2 * p, reach)
        step(spare, state, 2 * p + 1, reach)

    begin = 0
    for reach in range(HT, 0, -1):
        end = jnp.maximum(count - SUB * (reach - 1), 0) // 2
        lax.fori_loop(begin, end, functools.partial(pair, reach=reach), None)
        begin = end

    @pl.when(lax.rem(count, 2) == 1)
    def _():
        step(state, spare, count - 1, 0)
        for c in range(tiles):
            for r in range(strip_tiles):
                at = PAD + HALO + r * SUB
                state[c, at : at + SUB, :] = spare[c, at : at + SUB, :]


def with_halos(odd, got_a, got_b, place):
    @pl.when(odd)
    def _():
        place(got_a, True)
        place(got_b, False)

    @pl.when(jnp.logical_not(odd))
    def _():
        place(got_b, True)
        place(got_a, False)


def unpack(out, tiles, rows, payload, above, which, at=0):
    for c in range(tiles):
        if above:
            main, rest = at + HALO - MAIN, at + HALO - MAIN - REST
        else:
            main, rest = at + HALO + rows, at + HALO + rows + MAIN
        first = 3 * MAIN + which * REST
        out[c, main : main + MAIN, :] = payload[which * MAIN : (which + 1) * MAIN, cols(c)]
        out[c, rest : rest + REST, :] = payload[first : first + REST, cols(c)]


def first_body(
    point, rate, source, got_a, got_b, initial, own_blocks, steps_far, waveform_far,
    relaxed, edge_a, edge_b, weights, state, spare, force, rates, conduct, steps, waveform, sems,
):
    copies = fetch(((steps_far, steps), (waveform_far, waveform)), sems)
    rows, width = point.shape
    tiles, strip_tiles = width // LANES, rows // SUB
    every = 2 * HT + strip_tiles
    mine, strip = lax.axis_index("tm"), lax.axis_index("space")
    odd = lax.rem(strip, 2) == 1
    zero = jnp.zeros((SUB, LANES), F32)

    def block(row):
        return jnp.broadcast_to(row, (SUB, LANES))

    for c in range(tiles):
        for r in range(strip_tiles):
            at, to = slice(r * SUB, (r + 1) * SUB), slice(HALO + r * SUB, HALO + (r + 1) * SUB)
            state[c, PAD + HALO + r * SUB : PAD + HALO + (r + 1) * SUB, :] = point[at, cols(c)]
            rates[c, to, :] = rate[at, cols(c)]
            force[c, to, :] = source[at, cols(c)]
            conduct[c, to, :] = block(own_blocks[r : r + 1, cols(c)])
        for at in (0, HALO + rows + HALO - SUB):
            rates[c, at : at + SUB, :] = zero
            force[c, at : at + SUB, :] = zero
            state[c, PAD + at : PAD + at + SUB, :] = zero

    def place(payload, above):
        unpack(state, tiles, rows, payload, above, 0, PAD)
        unpack(rates, tiles, rows, payload, above, 1)
        unpack(force, tiles, rows, payload, above, 2)
        for b in range(HT):
            at = b * SUB + (0 if above else HALO + rows)
            row = 3 * MAIN + 3 * REST + b
            for c in range(tiles):
                conduct[c, at : at + SUB, :] = block(payload[row : row + 1, cols(c)])

    with_halos(odd, got_a, got_b, place)

    sub, lane = iota(0), iota(1)
    here = [conduct[c, 0:SUB, :] for c in range(tiles)]
    over = [zero] * tiles
    for r in range(every):
        if r + 1 < every:
            follow = [conduct[c, (r + 1) * SUB : (r + 2) * SUB, :] for c in range(tiles)]
            under = [jnp.sqrt(k * f) for k, f in zip(here, follow)]
        else:
            follow, under = here, [zero] * tiles
        sides = [zero] + [jnp.sqrt(here[c] * here[c + 1]) for c in range(tiles - 1)] + [zero]
        for c in range(tiles):
            own, k = rates[c, r * SUB : (r + 1) * SUB, :], here[c]
            w = [
                own * jnp.where(sub == 0, over[c], k),
                own * jnp.where(sub == SUB - 1, under[c], k),
                own * jnp.where(lane == 0, sides[c], k),
                own * jnp.where(lane == LANES - 1, sides[c + 1], k),
            ]
            weights[0, c, r * SUB : (r + 1) * SUB, :] = 1.0 - (((w[0] + w[1]) + w[2]) + w[3])
            for i in range(4):
                weights[i + 1, c, r * SUB : (r + 1) * SUB, :] = w[i]
        here, over = follow, under

    for copy in copies:
        copy.wait()
    start = lax.fori_loop(0, mine, lambda i, total: total + steps[i], jnp.int32(0))
    count = steps[mine]
    sweep(state, spare, weights, force, count, tiles, strip_tiles, lambda t: waveform[start + t])

    def give(read):
        for c in range(tiles):
            for r in range(strip_tiles):
                relaxed[r * SUB : (r + 1) * SUB, cols(c)] = read(r, c)

        @pl.when(odd)
        def _():
            for c in range(tiles):
                for r in range(HT):
                    edge_a[r * SUB : (r + 1) * SUB, cols(c)] = read(r, c)
                    edge_b[r * SUB : (r + 1) * SUB, cols(c)] = read(strip_tiles - HT + r, c)

        @pl.when(jnp.logical_not(odd))
        def _():
            for c in range(tiles):
                for r in range(HT):
                    edge_b[r * SUB : (r + 1) * SUB, cols(c)] = read(r, c)
                    edge_a[r * SUB : (r + 1) * SUB, cols(c)] = read(strip_tiles - HT + r, c)

    last = mine == lax.axis_size("tm") - 1

    @pl.when(last)
    def _():
        give(lambda r, c: initial[r * SUB : (r + 1) * SUB, cols(c)])

    @pl.when(jnp.logical_not(last))
    def _():
        give(lambda r, c: state[c, PAD + HALO + r * SUB : PAD + HALO + (r + 1) * SUB, :])


def second_body(
    relaxed, edge_a, edge_b, point, got_a, got_b, weights, steps_far, coarse, state, spare, tmp, steps, sems
):
    copies = fetch(((steps_far, steps),), sems)
    rows, width = point.shape
    tiles, strip_tiles = width // LANES, rows // SUB
    mine, strip = lax.axis_index("tm"), lax.axis_index("space")
    odd = lax.rem(strip, 2) == 1
    for c in range(tiles):
        for r in range(strip_tiles):
            at = slice(r * SUB, (r + 1) * SUB)
            to = PAD + HALO + r * SUB
            state[c, to : to + SUB, :] = relaxed[at, cols(c)] - point[at, cols(c)]
        for at in (0, HALO + rows + HALO - SUB):
            tmp[c, at : at + SUB, :] = jnp.zeros((SUB, LANES), F32)

    def place(pair, above):
        edge, payload = pair
        unpack(tmp, tiles, rows, payload, above, 0)
        base = 0 if above else HALO + rows
        for c in range(tiles):
            for r in range(HT):
                at = base + r * SUB
                state[c, PAD + at : PAD + at + SUB, :] = edge[r * SUB : (r + 1) * SUB, cols(c)] - tmp[c, at : at + SUB, :]

    with_halos(odd, (edge_a, got_a), (edge_b, got_b), place)
    copies[0].wait()
    count = steps[mine]
    sweep(state, spare, weights, None, count, tiles, strip_tiles, None)
    pairs = halve()
    for c in range(tiles // 2):
        wide = [row_pairs(state, (2 * c + k,), PAD + HALO, rows // 2) for k in (0, 1)]
        coarse[:, cols(c)] = 0.25 * dot(jnp.concatenate(wide, axis=1), pairs)


def assemble_body(strips, fields, total, weights, conduct):
    count = len(strips)
    rows, width = strips[0].shape
    tiles = width // LANES
    mine = lax.axis_index("space")
    per_block = BLK_R // 2
    zero = jnp.zeros((SUB, LANES), F32)
    for c in range(tiles):
        conduct[c, 0:PAD, :] = zero
        conduct[c, PAD + count * rows :, :] = zero
    for k in range(count):
        base = (mine ^ k) * rows
        for c in range(tiles):
            for r in range(rows // SUB):
                to = pl.multiple_of(base + r * SUB, SUB)
                total[c, pl.ds(to, SUB), :] = strips[k][r * SUB : (r + 1) * SUB, cols(c)]
                weights[0, c, pl.ds(to, SUB), :] = fields[k][r * SUB : (r + 1) * SUB, cols(c)]
                block = rows + r * (SUB // per_block)
                two = [jnp.broadcast_to(fields[k][block + i : block + i + 1, cols(c)], (SUB, LANES)) for i in (0, 1)]
                conduct[c, pl.ds(PAD + to, SUB), :] = jnp.where(iota(0) < per_block, two[0], two[1])
    for r in range(count * rows // SUB):
        at = PAD + r * SUB
        here = [conduct[c, at : at + SUB, :] for c in range(tiles)]
        for c in range(tiles):
            left, right = beside(here, c, zero)
            above = conduct[c, at - 1 : at + SUB - 1, :]
            below = conduct[c, at + 1 : at + SUB + 1, :]
            own = weights[0, c, r * SUB : (r + 1) * SUB, :]
            w = [own * jnp.sqrt(here[c] * other) for other in (above, below, left, right)]
            weights[0, c, r * SUB : (r + 1) * SUB, :] = ((w[0] + w[1]) + w[2]) + w[3]
            for k in range(4):
                weights[k + 1, c, r * SUB : (r + 1) * SUB, :] = w[k]


def link(buffers, weights, factor):
    state, one, two = buffers
    tiles, padded, _ = state.shape

    def step(source, target):
        for r in range((padded - 2 * PAD) // SUB):
            at = PAD + r * SUB
            here = [source[c, at : at + SUB, :] for c in range(tiles)]
            for c in range(tiles):
                left, right = beside(here, c)
                above = source[c, at - 1 : at + SUB - 1, :]
                below = source[c, at + 1 : at + SUB + 1, :]
                w = [weights[k, c, r * SUB : (r + 1) * SUB, :] for k in range(5)]
                change = (w[1] * above + w[2] * below) + (w[3] * left + w[4] * right) - w[0] * here[c]
                target[c, at : at + SUB, :] = here[c] + factor * change

    source = state
    for k in range(CSUB):
        target = state if k == CSUB - 1 else (two if source is one else one)
        step(source, target)
        source = target


def scan_body(stage, final, refs):
    total, got, before, weights, steps = refs[:5]
    tiles, height, _ = total.shape
    size = 1 << stage
    mine, strip = lax.axis_index("tm"), lax.axis_index("space")
    upper = lax.rem(mine // size, 2) == 1
    first = (mine // (2 * size)) * (2 * size) + size
    if final:
        relaxed, out, *buffers, errors, tmp = refs[5:]
        rows = 2 * relaxed.shape[0] // 4
    else:
        total_out, errors, *buffers = refs[5:]
        rows = errors.shape[1]
    mine_rows = pl.multiple_of(strip * rows, SUB)
    zero = jnp.zeros((SUB, LANES), F32)
    state = buffers[0]
    for c in range(tiles):
        for buffer in buffers:
            buffer[c, 0:PAD, :] = zero
            buffer[c, PAD + height :, :] = zero

    def load(ref):
        for c in range(tiles):
            for r in range(height // SUB):
                state[c, PAD + r * SUB : PAD + (r + 1) * SUB, :] = ref[c, r * SUB : (r + 1) * SUB, :]

    @pl.when(upper)
    def _():
        load(got)

    @pl.when(jnp.logical_not(upper))
    def _():
        load(total)

    def keep():
        for c in range(tiles):
            piece = state[c, pl.ds(PAD + mine_rows, rows), :]
            errors[c, :, :] = piece if before is None else before[c, :, :] + piece

    def pass_on():
        for c in range(tiles):
            if before is None:
                errors[c, :, :] = jnp.zeros((rows, LANES), F32)
            else:
                errors[c, :, :] = before[c, :, :]

    pass_on()

    def turn(i, _):
        @pl.when(jnp.logical_and(upper, first + i == mine))
        def _():
            keep()

        link(buffers, weights, steps[first + i].astype(F32) * (1.0 / (4.0 * CSUB)))

    if final:
        turns = jnp.where(upper, mine - first, 0)
        lax.fori_loop(0, turns, turn, None)

        @pl.when(upper)
        def _():
            keep()

        pairs = double()
        for c in range(tiles):
            wide = dot(errors[c, :, :], pairs)
            for k in (0, 1):
                part = wide[:, k * LANES : (k + 1) * LANES]
                tmp[2 * c + k, pl.ds(0, rows, stride=2), :] = part
                tmp[2 * c + k, pl.ds(1, rows, stride=2), :] = part
        for c in range(2 * tiles):
            out[:, cols(c)] = relaxed[:, cols(c)] + tmp[c, :, :]
    else:
        lax.fori_loop(0, size, turn, None)

        def close(ref):
            for c in range(tiles):
                for r in range(height // SUB):
                    at = slice(r * SUB, (r + 1) * SUB)
                    total_out[c, at, :] = ref[c, at, :] + state[c, PAD + r * SUB : PAD + (r + 1) * SUB, :]

        @pl.when(upper)
        def _():
            close(total)

        @pl.when(jnp.logical_not(upper))
        def _():
            close(got)


def shards(point_states, initial_state, node_rate, source_map, waveform, cond_table, class_map, interval_steps):
    assert point_states.shape[0] == 1
    intervals, strips = lax.axis_size("tm"), lax.axis_size("space")
    assert intervals & (intervals - 1) == 0 and strips & (strips - 1) == 0
    point = point_states[0]
    rows, width = point.shape
    tiles, ctiles, crows, blocks = width // LANES, width // LANES // 2, rows // 2, rows // BLK_R
    height, cheight = rows + 2 * HALO, crows * strips
    packed = -(-(3 * STEP_MOST + HT) // SUB) * SUB
    fields_rows = -(-(crows + blocks) // SUB) * SUB
    both = ("tm", "space")

    def side(s, which):
        other = s ^ 1 if which == "a" else (s + 1 if s % 2 else s - 1)
        return other if 0 <= other < strips else None

    def exchange(value, ahead, move):
        pairs = []
        for j in range(intervals):
            for s in range(strips):
                to = move(s)
                if to is not None:
                    pairs.append((j * strips + s, ((j + ahead) % intervals) * strips + to))
        return lax.ppermute(value, both, pairs)

    strip = f32(rows, width)
    pay_a, pay_b, field, own_blocks, point, rate, source, initial = call(
        pack_body, [FAR] * 6,
        (f32(packed, width), f32(packed, width), f32(fields_rows, width // 2), f32(SUB, width), strip, strip, strip, strip),
        [
            pltpu.SMEM(cond_table.shape, F32),
            pltpu.SMEM(class_map.shape, jnp.int32),
            pltpu.VMEM((tiles, rows, LANES), F32),
            pltpu.SemaphoreType.DMA((6,)),
        ],
        1 << 20,
    )(*[far(x) for x in (point, node_rate, source_map, initial_state, cond_table, class_map)])
    got_a = exchange(pay_a, 0, lambda s: side(s, "a"))
    got_b = exchange(pay_b, 0, lambda s: side(s, "b"))
    fields = [field]
    for k in range(1, strips):
        fields.append(exchange(field, 0, lambda s, k=k: s ^ k))

    grid = pltpu.VMEM((tiles, height + 2 * PAD, LANES), F32)
    flat = pltpu.VMEM((tiles, height, LANES), F32)
    steps_near = pltpu.SMEM(interval_steps.shape, jnp.int32)
    passed, edge_a, edge_b, weights = call(
        first_body, [VM] * 7 + [FAR] * 2,
        (strip, f32(HALO, width), f32(HALO, width), f32(5, tiles, height, LANES)),
        [grid, grid, flat, flat, flat, steps_near, pltpu.SMEM(waveform.shape, F32), pltpu.SemaphoreType.DMA((2,))],
        1 << 24,
    )(point, rate, source, got_a, got_b, initial, own_blocks, far(interval_steps), far(waveform))
    relaxed = exchange(passed, 1, lambda s: s)
    edge_a = exchange(edge_a, 1, lambda s: side(s, "a"))
    edge_b = exchange(edge_b, 1, lambda s: side(s, "b"))

    change = call(
        second_body, [VM] * 7 + [FAR], f32(crows, width // 2),
        [grid, grid, flat, steps_near, pltpu.SemaphoreType.DMA((1,))],
        1 << 24,
    )(relaxed, edge_a, edge_b, point, got_a, got_b, weights, far(interval_steps))
    changes = [change]
    for k in range(1, strips):
        changes.append(exchange(change, 0, lambda s, k=k: s ^ k))

    def assemble(*refs):
        assemble_body(refs[:strips], refs[strips : 2 * strips], *refs[2 * strips :])

    total, coarse_weights = call(
        assemble, [VM] * (2 * strips), (f32(ctiles, cheight, LANES), f32(5, ctiles, cheight, LANES)),
        [pltpu.VMEM((ctiles, cheight + 2 * PAD, LANES), F32)], 1 << 20,
    )(*changes, *fields)

    errors = None
    stages = intervals.bit_length() - 1
    for stage in range(stages):
        got = lax.ppermute(total, "tm", [(j, j ^ (1 << stage)) for j in range(intervals)])
        final = stage == stages - 1
        some = errors is not None

        def body(*refs, stage=stage, final=final, some=some):
            refs = refs if some else (*refs[:2], None, *refs[2:])
            scan_body(stage, final, refs)

        buffers = [pltpu.VMEM((ctiles, cheight + 2 * PAD, LANES), F32)] * 3
        lead = [total, got] + ([errors] if some else []) + [coarse_weights, interval_steps]
        specs = [VM] * (len(lead) - 1) + [SM]
        if final:
            out = call(
                body, specs + [VM], f32(rows, width),
                buffers + [pltpu.VMEM((ctiles, crows, LANES), F32), pltpu.VMEM((tiles, rows, LANES), F32)], 1 << 23,
            )(*lead, relaxed)
        else:
            total, errors = call(
                body, specs, (f32(ctiles, cheight, LANES), f32(ctiles, crows, LANES)), buffers, 1 << 23
            )(*lead)
    return out[None]


def solution(mesh):
    placed = (
        P("tm", "space", None),
        P("space", None),
        P("space", None),
        P("space", None),
        P(),
        P(),
        P("space", None),
        P(),
    )

    return jax.shard_map(shards, mesh=mesh, in_specs=placed, out_specs=P("tm", "space", None), check_vma=False)
```

```python
import functools

import jax
import jax.numpy as jnp
from jax import lax
from jax.experimental import pallas as pl
from jax.experimental.pallas import tpu as pltpu
from jax.sharding import PartitionSpec as P


STEP_MOST = 20
CSUB = 5
BLK_R = 8
SUB = 8
LANES = 128
MAIN = STEP_MOST // SUB * SUB
REST = STEP_MOST - MAIN
HALO = -(-STEP_MOST // SUB) * SUB
HT = HALO // SUB
PAD = SUB
VM = pl.BlockSpec(memory_space=pltpu.VMEM)
FAR = pl.BlockSpec(memory_space=pltpu.HBM)
F32 = jnp.float32
GRANT = 16 << 20


def f32(*shape):
    return jax.ShapeDtypeStruct(shape, F32)


def call(body, ins, outs, scratch, flops):
    return pl.pallas_call(
        body,
        out_shape=outs,
        in_specs=ins,
        out_specs=jax.tree.map(lambda _: VM, outs),
        scratch_shapes=scratch,
        compiler_params=pltpu.CompilerParams(vmem_limit_bytes=GRANT),
        cost_estimate=pl.CostEstimate(flops=flops, bytes_accessed=1 << 20, transcendentals=0),
    )


def far(value):
    return pltpu.with_memory_space_constraint(value, pltpu.HBM)


def iota(axis, shape=(SUB, LANES)):
    return lax.broadcasted_iota(jnp.int32, shape, axis)


def cols(c):
    return slice(c * LANES, (c + 1) * LANES)


def beside(tiles, c, left_edge=None):
    lane = iota(1)
    before = pltpu.roll(tiles[c], 1, 1)
    after = pltpu.roll(tiles[c], LANES - 1, 1)
    if c > 0:
        before = jnp.where(lane == 0, pltpu.roll(tiles[c - 1], 1, 1), before)
    elif left_edge is not None:
        before = jnp.where(lane == 0, left_edge, before)
    if c + 1 < len(tiles):
        after = jnp.where(lane == LANES - 1, pltpu.roll(tiles[c + 1], LANES - 1, 1), after)
    elif left_edge is not None:
        after = jnp.where(lane == LANES - 1, left_edge, after)
    return before, after


def halve():
    wide, narrow = iota(0, (2 * LANES, LANES)), iota(1, (2 * LANES, LANES))
    return jnp.where(wide // 2 == narrow, 1.0, 0.0).astype(F32)


def double():
    narrow, wide = iota(0, (LANES, 2 * LANES)), iota(1, (LANES, 2 * LANES))
    return jnp.where(wide // 2 == narrow, 1.0, 0.0).astype(F32)


def dot(a, b):
    return jnp.dot(a, b, precision=lax.Precision.HIGHEST, preferred_element_type=F32)


def row_pairs(ref, index, first, rows):
    top = ref[(*index, pl.ds(first, rows, stride=2), slice(None))]
    return top + ref[(*index, pl.ds(first + 1, rows, stride=2), slice(None))]


def fetch(pairs, sems):
    copies = [pltpu.make_async_copy(source, target, sems.at[i]) for i, (source, target) in enumerate(pairs)]
    for copy in copies:
        copy.start()
    return copies


def pack_body(
    point_far, rate_far, source_far, initial_far, table_far, classes_far,
    pay_a, pay_b, coarse, blocks_out, point, rate, source, initial, table, classes, tmp, sems,
):
    copies = fetch(
        (
            (table_far, table), (classes_far, classes), (rate_far, rate),
            (point_far, point), (source_far, source), (initial_far, initial),
        ), sems,
    )
    rows, width = point.shape
    blocks, tiles = rows // BLK_R, width // LANES
    odd = lax.rem(lax.axis_index("space"), 2) == 1
    copies[0].wait()
    copies[1].wait()
    for b in range(blocks):
        for c in range(tiles):
            blocks_out[b : b + 1, cols(c)] = jnp.full((1, LANES), table[classes[b, c]], F32)
    for copy in copies[2:5]:
        copy.wait()

    def fill(out, high):
        main = rows - MAIN if high else 0
        rest = rows - MAIN - REST if high else MAIN
        for i, ref in enumerate((point, rate, source)):
            out[i * MAIN : (i + 1) * MAIN, :] = ref[main : main + MAIN, :]
            at = 3 * MAIN + i * REST
            out[at : at + REST, :] = ref[rest : rest + REST, :]
        first = blocks - HT if high else 0
        at = 3 * MAIN + 3 * REST
        out[at : at + HT, :] = blocks_out[first : first + HT, :]

    @pl.when(odd)
    def _():
        fill(pay_a, False)
        fill(pay_b, True)

    @pl.when(jnp.logical_not(odd))
    def _():
        fill(pay_a, True)
        fill(pay_b, False)

    for c in range(tiles):
        tmp[c, :, :] = rate[:, cols(c)]
    pairs = halve()
    for c in range(tiles // 2):
        wide = jnp.concatenate([row_pairs(tmp, (2 * c + k,), 0, rows // 2) for k in (0, 1)], axis=1)
        coarse[c * (rows // 2) : (c + 1) * (rows // 2), :] = 0.25 * dot(wide, pairs)
        halves = [blocks_out[0:blocks, cols(2 * c + k)] for k in (0, 1)]
        at = tiles // 2 * (rows // 2) + c * blocks
        coarse[at : at + blocks, :] = jnp.where(
            iota(1, (blocks, LANES)) < LANES // 2, halves[0], halves[1]
        )
    copies[5].wait()


def sweep(state, spare, weights, force, count, tiles, strip_tiles, wave):
    def step(source, target, t, reach):
        amount = None if wave is None else wave(t)
        for r in range(HT - reach, HT + strip_tiles + reach):
            at = PAD + r * SUB
            here = [source[c, at : at + SUB, :] for c in range(tiles)]
            for c in range(tiles):
                left, right = beside(here, c)
                above = source[c, at - 1 : at + SUB - 1, :]
                below = source[c, at + 1 : at + SUB + 1, :]
                w = [weights[k, c, r * SUB : (r + 1) * SUB, :] for k in range(5)]
                new = (w[0] * here[c] + w[1] * above) + (w[2] * below + w[3] * left) + w[4] * right
                if amount is not None:
                    new = new + amount * force[c, r * SUB : (r + 1) * SUB, :]
                target[c, at : at + SUB, :] = new

    def pair(p, _, reach):
        step(state, spare, 2 * p, reach)
        step(spare, state, 2 * p + 1, reach)

    begin = 0
    for reach in range(HT, 0, -1):
        end = jnp.maximum(count - SUB * (reach - 1), 0) // 2
        lax.fori_loop(begin, end, functools.partial(pair, reach=reach), None)
        begin = end

    @pl.when(lax.rem(count, 2) == 1)
    def _():
        step(state, spare, count - 1, 0)
        for c in range(tiles):
            for r in range(strip_tiles):
                at = PAD + HALO + r * SUB
                state[c, at : at + SUB, :] = spare[c, at : at + SUB, :]


def with_halos(odd, got_a, got_b, place):
    @pl.when(odd)
    def _():
        place(got_a, True)
        place(got_b, False)

    @pl.when(jnp.logical_not(odd))
    def _():
        place(got_b, True)
        place(got_a, False)


def unpack(out, tiles, rows, payload, above, which, at=0):
    for c in range(tiles):
        if above:
            main, rest = at + HALO - MAIN, at + HALO - MAIN - REST
        else:
            main, rest = at + HALO + rows, at + HALO + rows + MAIN
        first = 3 * MAIN + which * REST
        out[c, main : main + MAIN, :] = payload[which * MAIN : (which + 1) * MAIN, cols(c)]
        out[c, rest : rest + REST, :] = payload[first : first + REST, cols(c)]


def first_body(
    point, rate, source, got_a, got_b, initial, own_blocks, steps_far, waveform_far,
    relaxed, edge_a, edge_b, weights, factors, state, spare, force, rates, conduct, steps, waveform, sems,
):
    copies = fetch(((steps_far, steps), (waveform_far, waveform)), sems)
    rows, width = point.shape
    tiles, strip_tiles = width // LANES, rows // SUB
    every = 2 * HT + strip_tiles
    mine, strip = lax.axis_index("tm"), lax.axis_index("space")
    odd = lax.rem(strip, 2) == 1
    zero = jnp.zeros((SUB, LANES), F32)

    def block(row):
        return jnp.broadcast_to(row, (SUB, LANES))

    for c in range(tiles):
        for r in range(strip_tiles):
            at, to = slice(r * SUB, (r + 1) * SUB), slice(HALO + r * SUB, HALO + (r + 1) * SUB)
            state[c, PAD + HALO + r * SUB : PAD + HALO + (r + 1) * SUB, :] = point[at, cols(c)]
            rates[c, to, :] = rate[at, cols(c)]
            force[c, to, :] = source[at, cols(c)]
            conduct[c, to, :] = block(own_blocks[r : r + 1, cols(c)])
        for at in (0, HALO + rows + HALO - SUB):
            rates[c, at : at + SUB, :] = zero
            force[c, at : at + SUB, :] = zero
            state[c, PAD + at : PAD + at + SUB, :] = zero

    def place(payload, above):
        unpack(state, tiles, rows, payload, above, 0, PAD)
        unpack(rates, tiles, rows, payload, above, 1)
        unpack(force, tiles, rows, payload, above, 2)
        for b in range(HT):
            at = b * SUB + (0 if above else HALO + rows)
            row = 3 * MAIN + 3 * REST + b
            for c in range(tiles):
                conduct[c, at : at + SUB, :] = block(payload[row : row + 1, cols(c)])

    with_halos(odd, got_a, got_b, place)

    sub, lane = iota(0), iota(1)
    here = [conduct[c, 0:SUB, :] for c in range(tiles)]
    over = [zero] * tiles
    for r in range(every):
        if r + 1 < every:
            follow = [conduct[c, (r + 1) * SUB : (r + 2) * SUB, :] for c in range(tiles)]
            under = [jnp.sqrt(k * f) for k, f in zip(here, follow)]
        else:
            follow, under = here, [zero] * tiles
        sides = [zero] + [jnp.sqrt(here[c] * here[c + 1]) for c in range(tiles - 1)] + [zero]
        for c in range(tiles):
            own, k = rates[c, r * SUB : (r + 1) * SUB, :], here[c]
            w = [
                own * jnp.where(sub == 0, over[c], k),
                own * jnp.where(sub == SUB - 1, under[c], k),
                own * jnp.where(lane == 0, sides[c], k),
                own * jnp.where(lane == LANES - 1, sides[c + 1], k),
            ]
            weights[0, c, r * SUB : (r + 1) * SUB, :] = 1.0 - (((w[0] + w[1]) + w[2]) + w[3])
            for i in range(4):
                weights[i + 1, c, r * SUB : (r + 1) * SUB, :] = w[i]
        here, over = follow, under

    for copy in copies:
        copy.wait()
    start = lax.fori_loop(0, mine, lambda i, total: total + steps[i], jnp.int32(0))
    count = steps[mine]
    for i in range(steps.shape[0]):
        value = steps[i].astype(F32) * (1.0 / (4.0 * CSUB))
        factors[i : i + 1, :] = jnp.full((1, LANES), value, F32)
    sweep(state, spare, weights, force, count, tiles, strip_tiles, lambda t: waveform[start + t])

    def give(read):
        for c in range(tiles):
            for r in range(strip_tiles):
                relaxed[r * SUB : (r + 1) * SUB, cols(c)] = read(r, c)

        @pl.when(odd)
        def _():
            for c in range(tiles):
                for r in range(HT):
                    edge_a[r * SUB : (r + 1) * SUB, cols(c)] = read(r, c)
                    edge_b[r * SUB : (r + 1) * SUB, cols(c)] = read(strip_tiles - HT + r, c)

        @pl.when(jnp.logical_not(odd))
        def _():
            for c in range(tiles):
                for r in range(HT):
                    edge_b[r * SUB : (r + 1) * SUB, cols(c)] = read(r, c)
                    edge_a[r * SUB : (r + 1) * SUB, cols(c)] = read(strip_tiles - HT + r, c)

    last = mine == lax.axis_size("tm") - 1

    @pl.when(last)
    def _():
        give(lambda r, c: initial[r * SUB : (r + 1) * SUB, cols(c)])

    @pl.when(jnp.logical_not(last))
    def _():
        give(lambda r, c: state[c, PAD + HALO + r * SUB : PAD + HALO + (r + 1) * SUB, :])


def second_body(
    relaxed, edge_a, edge_b, point, got_a, got_b, weights, steps_far, coarse, state, spare, tmp, steps, sems
):
    copies = fetch(((steps_far, steps),), sems)
    rows, width = point.shape
    tiles, strip_tiles = width // LANES, rows // SUB
    mine, strip = lax.axis_index("tm"), lax.axis_index("space")
    odd = lax.rem(strip, 2) == 1
    for c in range(tiles):
        for r in range(strip_tiles):
            at = slice(r * SUB, (r + 1) * SUB)
            to = PAD + HALO + r * SUB
            state[c, to : to + SUB, :] = relaxed[at, cols(c)] - point[at, cols(c)]
        for at in (0, HALO + rows + HALO - SUB):
            tmp[c, at : at + SUB, :] = jnp.zeros((SUB, LANES), F32)

    def place(pair, above):
        edge, payload = pair
        unpack(tmp, tiles, rows, payload, above, 0)
        base = 0 if above else HALO + rows
        for c in range(tiles):
            for r in range(HT):
                at = base + r * SUB
                state[c, PAD + at : PAD + at + SUB, :] = edge[r * SUB : (r + 1) * SUB, cols(c)] - tmp[c, at : at + SUB, :]

    with_halos(odd, (edge_a, got_a), (edge_b, got_b), place)
    copies[0].wait()
    count = steps[mine]
    sweep(state, spare, weights, None, count, tiles, strip_tiles, None)
    pairs = halve()
    for c in range(tiles // 2):
        wide = [row_pairs(state, (2 * c + k,), PAD + HALO, rows // 2) for k in (0, 1)]
        coarse[:, cols(c)] = 0.25 * dot(jnp.concatenate(wide, axis=1), pairs)


def assemble_body(strips, fields, total, weights, conduct):
    count = len(strips)
    rows, width = strips[0].shape
    tiles = width // LANES
    mine = lax.axis_index("space")
    per_block = BLK_R // 2
    zero = jnp.zeros((SUB, LANES), F32)
    for c in range(tiles):
        conduct[c, 0:PAD, :] = zero
        conduct[c, PAD + count * rows :, :] = zero
    for k in range(count):
        base = (mine ^ k) * rows
        for c in range(tiles):
            for r in range(rows // SUB):
                to = pl.multiple_of(base + r * SUB, SUB)
                total[c, pl.ds(to, SUB), :] = strips[k][r * SUB : (r + 1) * SUB, cols(c)]
                weights[0, c, pl.ds(to, SUB), :] = fields[k][c * rows + r * SUB : c * rows + (r + 1) * SUB, :]
                block = tiles * rows + c * (rows // per_block) + r * (SUB // per_block)
                two = [jnp.broadcast_to(fields[k][block + i : block + i + 1, :], (SUB, LANES)) for i in (0, 1)]
                conduct[c, pl.ds(PAD + to, SUB), :] = jnp.where(iota(0) < per_block, two[0], two[1])
    for r in range(count * rows // SUB):
        at = PAD + r * SUB
        here = [conduct[c, at : at + SUB, :] for c in range(tiles)]
        for c in range(tiles):
            left, right = beside(here, c, zero)
            above = conduct[c, at - 1 : at + SUB - 1, :]
            below = conduct[c, at + 1 : at + SUB + 1, :]
            own = weights[0, c, r * SUB : (r + 1) * SUB, :]
            w = [own * jnp.sqrt(here[c] * other) for other in (above, below, left, right)]
            weights[0, c, r * SUB : (r + 1) * SUB, :] = ((w[0] + w[1]) + w[2]) + w[3]
            for k in range(4):
                weights[k + 1, c, r * SUB : (r + 1) * SUB, :] = w[k]


def link(buffers, weights, factor):
    state, one, two = buffers
    tiles, padded, _ = state.shape

    def step(source, target):
        for r in range((padded - 2 * PAD) // SUB):
            at = PAD + r * SUB
            here = [source[c, at : at + SUB, :] for c in range(tiles)]
            for c in range(tiles):
                left, right = beside(here, c)
                above = source[c, at - 1 : at + SUB - 1, :]
                below = source[c, at + 1 : at + SUB + 1, :]
                w = [weights[k, c, r * SUB : (r + 1) * SUB, :] for k in range(5)]
                change = (w[1] * above + w[2] * below) + (w[3] * left + w[4] * right) - w[0] * here[c]
                target[c, at : at + SUB, :] = here[c] + factor * change

    source = state
    for k in range(CSUB):
        target = state if k == CSUB - 1 else (two if source is one else one)
        step(source, target)
        source = target


def scan_body(stage, final, refs):
    total, got, before, weights, factors = refs[:5]
    tiles, height, _ = total.shape
    size = 1 << stage
    mine, strip = lax.axis_index("tm"), lax.axis_index("space")
    upper = lax.rem(mine // size, 2) == 1
    first = (mine // (2 * size)) * (2 * size) + size
    if final:
        relaxed, out, *buffers, errors, tmp = refs[5:]
        rows = 2 * relaxed.shape[0] // 4
    else:
        total_out, errors, *buffers = refs[5:]
        rows = errors.shape[1]
    mine_rows = pl.multiple_of(strip * rows, SUB)
    zero = jnp.zeros((SUB, LANES), F32)
    state = buffers[0]
    for c in range(tiles):
        for buffer in buffers:
            buffer[c, 0:PAD, :] = zero
            buffer[c, PAD + height :, :] = zero

    def load(ref):
        for c in range(tiles):
            for r in range(height // SUB):
                state[c, PAD + r * SUB : PAD + (r + 1) * SUB, :] = ref[c, r * SUB : (r + 1) * SUB, :]

    @pl.when(upper)
    def _():
        load(got)

    @pl.when(jnp.logical_not(upper))
    def _():
        load(total)

    def keep():
        for c in range(tiles):
            piece = state[c, pl.ds(PAD + mine_rows, rows), :]
            errors[c, :, :] = piece if before is None else before[c, :, :] + piece

    def pass_on():
        for c in range(tiles):
            if before is None:
                errors[c, :, :] = jnp.zeros((rows, LANES), F32)
            else:
                errors[c, :, :] = before[c, :, :]

    pass_on()

    def turn(i, _):
        @pl.when(jnp.logical_and(upper, first + i == mine))
        def _():
            keep()

        link(buffers, weights, jnp.broadcast_to(factors[pl.ds(first + i, 1), :], (SUB, LANES)))

    if final:
        turns = jnp.where(upper, mine - first, 0)
        lax.fori_loop(0, turns, turn, None)

        @pl.when(upper)
        def _():
            keep()

        pairs = double()
        for c in range(tiles):
            wide = dot(errors[c, :, :], pairs)
            for k in (0, 1):
                part = wide[:, k * LANES : (k + 1) * LANES]
                tmp[2 * c + k, pl.ds(0, rows, stride=2), :] = part
                tmp[2 * c + k, pl.ds(1, rows, stride=2), :] = part
        for c in range(2 * tiles):
            out[:, cols(c)] = relaxed[:, cols(c)] + tmp[c, :, :]
    else:
        lax.fori_loop(0, size, turn, None)

        def close(ref):
            for c in range(tiles):
                for r in range(height // SUB):
                    at = slice(r * SUB, (r + 1) * SUB)
                    total_out[c, at, :] = ref[c, at, :] + state[c, PAD + r * SUB : PAD + (r + 1) * SUB, :]

        @pl.when(upper)
        def _():
            close(total)

        @pl.when(jnp.logical_not(upper))
        def _():
            close(got)


def shards(point_states, initial_state, node_rate, source_map, waveform, cond_table, class_map, interval_steps):
    assert point_states.shape[0] == 1
    intervals, strips = lax.axis_size("tm"), lax.axis_size("space")
    assert intervals & (intervals - 1) == 0 and strips & (strips - 1) == 0
    point = point_states[0]
    rows, width = point.shape
    tiles, ctiles, crows, blocks = width // LANES, width // LANES // 2, rows // 2, rows // BLK_R
    height, cheight = rows + 2 * HALO, crows * strips
    packed = -(-(3 * STEP_MOST + HT) // SUB) * SUB
    fields_rows = -(-ctiles * (crows + blocks) // SUB) * SUB
    both = ("tm", "space")

    def side(s, which):
        other = s ^ 1 if which == "a" else (s + 1 if s % 2 else s - 1)
        return other if 0 <= other < strips else None

    def exchange(value, ahead, move):
        pairs = []
        for j in range(intervals):
            for s in range(strips):
                to = move(s)
                if to is not None:
                    pairs.append((j * strips + s, ((j + ahead) % intervals) * strips + to))
        return lax.ppermute(value, both, pairs)

    strip = f32(rows, width)
    pay_a, pay_b, field, own_blocks, point, rate, source, initial = call(
        pack_body, [FAR] * 6,
        (f32(packed, width), f32(packed, width), f32(fields_rows, LANES), f32(SUB, width), strip, strip, strip, strip),
        [
            pltpu.SMEM(cond_table.shape, F32),
            pltpu.SMEM(class_map.shape, jnp.int32),
            pltpu.VMEM((tiles, rows, LANES), F32),
            pltpu.SemaphoreType.DMA((6,)),
        ],
        1 << 20,
    )(*[far(x) for x in (point, node_rate, source_map, initial_state, cond_table, class_map)])
    got_a = exchange(pay_a, 0, lambda s: side(s, "a"))
    got_b = exchange(pay_b, 0, lambda s: side(s, "b"))
    fields = [field]
    for k in range(1, strips):
        fields.append(exchange(field, 0, lambda s, k=k: s ^ k))

    grid = pltpu.VMEM((tiles, height + 2 * PAD, LANES), F32)
    flat = pltpu.VMEM((tiles, height, LANES), F32)
    steps_near = pltpu.SMEM(interval_steps.shape, jnp.int32)
    passed, edge_a, edge_b, weights, factors = call(
        first_body, [VM] * 7 + [FAR] * 2,
        (strip, f32(HALO, width), f32(HALO, width), f32(5, tiles, height, LANES), f32(-(-intervals // SUB) * SUB, LANES)),
        [grid, grid, flat, flat, flat, steps_near, pltpu.SMEM(waveform.shape, F32), pltpu.SemaphoreType.DMA((2,))],
        1 << 24,
    )(point, rate, source, got_a, got_b, initial, own_blocks, far(interval_steps), far(waveform))
    relaxed = exchange(passed, 1, lambda s: s)
    edge_a = exchange(edge_a, 1, lambda s: side(s, "a"))
    edge_b = exchange(edge_b, 1, lambda s: side(s, "b"))

    change = call(
        second_body, [VM] * 7 + [FAR], f32(crows, width // 2),
        [grid, grid, flat, steps_near, pltpu.SemaphoreType.DMA((1,))],
        1 << 24,
    )(relaxed, edge_a, edge_b, point, got_a, got_b, weights, far(interval_steps))
    changes = [change]
    for k in range(1, strips):
        changes.append(exchange(change, 0, lambda s, k=k: s ^ k))

    def assemble(*refs):
        assemble_body(refs[:strips], refs[strips : 2 * strips], *refs[2 * strips :])

    total, coarse_weights = call(
        assemble, [VM] * (2 * strips), (f32(ctiles, cheight, LANES), f32(5, ctiles, cheight, LANES)),
        [pltpu.VMEM((ctiles, cheight + 2 * PAD, LANES), F32)], 1 << 20,
    )(*changes, *fields)

    errors = None
    stages = intervals.bit_length() - 1
    for stage in range(stages):
        got = lax.ppermute(total, "tm", [(j, j ^ (1 << stage)) for j in range(intervals)])
        final = stage == stages - 1
        some = errors is not None

        def body(*refs, stage=stage, final=final, some=some):
            refs = refs if some else (*refs[:2], None, *refs[2:])
            scan_body(stage, final, refs)

        buffers = [pltpu.VMEM((ctiles, cheight + 2 * PAD, LANES), F32)] * 3
        lead = [total, got] + ([errors] if some else []) + [coarse_weights, factors]
        specs = [VM] * len(lead)
        if final:
            out = call(
                body, specs + [VM], f32(rows, width),
                buffers + [pltpu.VMEM((ctiles, crows, LANES), F32), pltpu.VMEM((tiles, rows, LANES), F32)], 1 << 23,
            )(*lead, relaxed)
        else:
            total, errors = call(
                body, specs, (f32(ctiles, cheight, LANES), f32(ctiles, crows, LANES)), buffers, 1 << 23
            )(*lead)
    return out[None]


def solution(mesh):
    placed = (
        P("tm", "space", None),
        P("space", None),
        P("space", None),
        P("space", None),
        P(),
        P(),
        P("space", None),
        P(),
    )

    return jax.shard_map(shards, mesh=mesh, in_specs=placed, out_specs=P("tm", "space", None), check_vma=False)
```

```python
import functools

import jax
import jax.numpy as jnp
from jax import lax
from jax.experimental import pallas as pl
from jax.experimental.pallas import tpu as pltpu
from jax.sharding import PartitionSpec as P


STEP_MOST = 20
CSUB = 5
BLK_R = 8
SUB = 8
LANES = 128
MAIN = STEP_MOST // SUB * SUB
REST = STEP_MOST - MAIN
HALO = -(-STEP_MOST // SUB) * SUB
HT = HALO // SUB
PAD = SUB
VM = pl.BlockSpec(memory_space=pltpu.VMEM)
FAR = pl.BlockSpec(memory_space=pltpu.HBM)
F32 = jnp.float32
GRANT = 16 << 20


def f32(*shape):
    return jax.ShapeDtypeStruct(shape, F32)


def call(body, ins, outs, scratch, flops):
    return pl.pallas_call(
        body,
        out_shape=outs,
        in_specs=ins,
        out_specs=jax.tree.map(lambda _: VM, outs),
        scratch_shapes=scratch,
        compiler_params=pltpu.CompilerParams(vmem_limit_bytes=GRANT),
        cost_estimate=pl.CostEstimate(flops=flops, bytes_accessed=1 << 20, transcendentals=0),
    )


def far(value):
    return pltpu.with_memory_space_constraint(value, pltpu.HBM)


def iota(axis, shape=(SUB, LANES)):
    return lax.broadcasted_iota(jnp.int32, shape, axis)


def cols(c):
    return slice(c * LANES, (c + 1) * LANES)


def beside(tiles, c, left_edge=None):
    lane = iota(1)
    before = pltpu.roll(tiles[c], 1, 1)
    after = pltpu.roll(tiles[c], LANES - 1, 1)
    if c > 0:
        before = jnp.where(lane == 0, pltpu.roll(tiles[c - 1], 1, 1), before)
    elif left_edge is not None:
        before = jnp.where(lane == 0, left_edge, before)
    if c + 1 < len(tiles):
        after = jnp.where(lane == LANES - 1, pltpu.roll(tiles[c + 1], LANES - 1, 1), after)
    elif left_edge is not None:
        after = jnp.where(lane == LANES - 1, left_edge, after)
    return before, after


def halve():
    wide, narrow = iota(0, (2 * LANES, LANES)), iota(1, (2 * LANES, LANES))
    return jnp.where(wide // 2 == narrow, 1.0, 0.0).astype(F32)


def double():
    narrow, wide = iota(0, (LANES, 2 * LANES)), iota(1, (LANES, 2 * LANES))
    return jnp.where(wide // 2 == narrow, 1.0, 0.0).astype(F32)


def dot(a, b):
    return jnp.dot(a, b, precision=lax.Precision.HIGHEST, preferred_element_type=F32)


def row_pairs(ref, index, first, rows):
    top = ref[(*index, pl.ds(first, rows, stride=2), slice(None))]
    return top + ref[(*index, pl.ds(first + 1, rows, stride=2), slice(None))]


def fetch(pairs, sems):
    copies = [pltpu.make_async_copy(source, target, sems.at[i]) for i, (source, target) in enumerate(pairs)]
    for copy in copies:
        copy.start()
    return copies


def pack_body(
    point_far, rate_far, source_far, initial_far, table_far, classes_far,
    pay_a, pay_b, blocks_out, point, rate, source, initial, table, classes, sems,
):
    copies = fetch(
        (
            (table_far, table), (classes_far, classes), (rate_far, rate),
            (point_far, point), (source_far, source), (initial_far, initial),
        ), sems,
    )
    rows, width = point.shape
    blocks, tiles = rows // BLK_R, width // LANES
    odd = lax.rem(lax.axis_index("space"), 2) == 1
    copies[0].wait()
    copies[1].wait()
    for b in range(blocks):
        for c in range(tiles):
            blocks_out[b : b + 1, cols(c)] = jnp.full((1, LANES), table[classes[b, c]], F32)
    for copy in copies[2:5]:
        copy.wait()

    def fill(out, high):
        main = rows - MAIN if high else 0
        rest = rows - MAIN - REST if high else MAIN
        for i, ref in enumerate((point, rate, source)):
            out[i * MAIN : (i + 1) * MAIN, :] = ref[main : main + MAIN, :]
            at = 3 * MAIN + i * REST
            out[at : at + REST, :] = ref[rest : rest + REST, :]
        first = blocks - HT if high else 0
        at = 3 * MAIN + 3 * REST
        out[at : at + HT, :] = blocks_out[first : first + HT, :]

    @pl.when(odd)
    def _():
        fill(pay_a, False)
        fill(pay_b, True)

    @pl.when(jnp.logical_not(odd))
    def _():
        fill(pay_a, True)
        fill(pay_b, False)

    copies[5].wait()


def coarsen_body(rate, blocks_out, coarse, tmp):
    rows, width = rate.shape
    blocks, tiles = rows // BLK_R, width // LANES
    for c in range(tiles):
        tmp[c, :, :] = rate[:, cols(c)]
    pairs = halve()
    for c in range(tiles // 2):
        wide = jnp.concatenate([row_pairs(tmp, (2 * c + k,), 0, rows // 2) for k in (0, 1)], axis=1)
        coarse[c * (rows // 2) : (c + 1) * (rows // 2), :] = 0.25 * dot(wide, pairs)
        halves = [blocks_out[0:blocks, cols(2 * c + k)] for k in (0, 1)]
        at = tiles // 2 * (rows // 2) + c * blocks
        coarse[at : at + blocks, :] = jnp.where(
            iota(1, (blocks, LANES)) < LANES // 2, halves[0], halves[1]
        )


def sweep(state, spare, weights, force, count, tiles, strip_tiles, wave):
    def step(source, target, t, reach):
        amount = None if wave is None else wave(t)
        for r in range(HT - reach, HT + strip_tiles + reach):
            at = PAD + r * SUB
            here = [source[c, at : at + SUB, :] for c in range(tiles)]
            for c in range(tiles):
                left, right = beside(here, c)
                above = source[c, at - 1 : at + SUB - 1, :]
                below = source[c, at + 1 : at + SUB + 1, :]
                w = [weights[k, c, r * SUB : (r + 1) * SUB, :] for k in range(5)]
                new = (w[0] * here[c] + w[1] * above) + (w[2] * below + w[3] * left) + w[4] * right
                if amount is not None:
                    new = new + amount * force[c, r * SUB : (r + 1) * SUB, :]
                target[c, at : at + SUB, :] = new

    def pair(p, _, reach):
        step(state, spare, 2 * p, reach)
        step(spare, state, 2 * p + 1, reach)

    begin = 0
    for reach in range(HT, 0, -1):
        end = jnp.maximum(count - SUB * (reach - 1), 0) // 2
        lax.fori_loop(begin, end, functools.partial(pair, reach=reach), None)
        begin = end

    @pl.when(lax.rem(count, 2) == 1)
    def _():
        step(state, spare, count - 1, 0)
        for c in range(tiles):
            for r in range(strip_tiles):
                at = PAD + HALO + r * SUB
                state[c, at : at + SUB, :] = spare[c, at : at + SUB, :]


def with_halos(odd, got_a, got_b, place):
    @pl.when(odd)
    def _():
        place(got_a, True)
        place(got_b, False)

    @pl.when(jnp.logical_not(odd))
    def _():
        place(got_b, True)
        place(got_a, False)


def unpack(out, tiles, rows, payload, above, which, at=0):
    for c in range(tiles):
        if above:
            main, rest = at + HALO - MAIN, at + HALO - MAIN - REST
        else:
            main, rest = at + HALO + rows, at + HALO + rows + MAIN
        first = 3 * MAIN + which * REST
        out[c, main : main + MAIN, :] = payload[which * MAIN : (which + 1) * MAIN, cols(c)]
        out[c, rest : rest + REST, :] = payload[first : first + REST, cols(c)]


def first_body(
    point, rate, source, got_a, got_b, initial, own_blocks, steps_far, waveform_far,
    relaxed, edge_a, edge_b, weights, factors, state, spare, force, rates, conduct, steps, waveform, sems,
):
    copies = fetch(((steps_far, steps), (waveform_far, waveform)), sems)
    rows, width = point.shape
    tiles, strip_tiles = width // LANES, rows // SUB
    every = 2 * HT + strip_tiles
    mine, strip = lax.axis_index("tm"), lax.axis_index("space")
    odd = lax.rem(strip, 2) == 1
    zero = jnp.zeros((SUB, LANES), F32)

    def block(row):
        return jnp.broadcast_to(row, (SUB, LANES))

    for c in range(tiles):
        for r in range(strip_tiles):
            at, to = slice(r * SUB, (r + 1) * SUB), slice(HALO + r * SUB, HALO + (r + 1) * SUB)
            state[c, PAD + HALO + r * SUB : PAD + HALO + (r + 1) * SUB, :] = point[at, cols(c)]
            rates[c, to, :] = rate[at, cols(c)]
            force[c, to, :] = source[at, cols(c)]
            conduct[c, to, :] = block(own_blocks[r : r + 1, cols(c)])
        for at in (0, HALO + rows + HALO - SUB):
            rates[c, at : at + SUB, :] = zero
            force[c, at : at + SUB, :] = zero
            state[c, PAD + at : PAD + at + SUB, :] = zero

    def place(payload, above):
        unpack(state, tiles, rows, payload, above, 0, PAD)
        unpack(rates, tiles, rows, payload, above, 1)
        unpack(force, tiles, rows, payload, above, 2)
        for b in range(HT):
            at = b * SUB + (0 if above else HALO + rows)
            row = 3 * MAIN + 3 * REST + b
            for c in range(tiles):
                conduct[c, at : at + SUB, :] = block(payload[row : row + 1, cols(c)])

    with_halos(odd, got_a, got_b, place)

    sub, lane = iota(0), iota(1)
    here = [conduct[c, 0:SUB, :] for c in range(tiles)]
    over = [zero] * tiles
    for r in range(every):
        if r + 1 < every:
            follow = [conduct[c, (r + 1) * SUB : (r + 2) * SUB, :] for c in range(tiles)]
            under = [jnp.sqrt(k * f) for k, f in zip(here, follow)]
        else:
            follow, under = here, [zero] * tiles
        sides = [zero] + [jnp.sqrt(here[c] * here[c + 1]) for c in range(tiles - 1)] + [zero]
        for c in range(tiles):
            own, k = rates[c, r * SUB : (r + 1) * SUB, :], here[c]
            w = [
                own * jnp.where(sub == 0, over[c], k),
                own * jnp.where(sub == SUB - 1, under[c], k),
                own * jnp.where(lane == 0, sides[c], k),
                own * jnp.where(lane == LANES - 1, sides[c + 1], k),
            ]
            weights[0, c, r * SUB : (r + 1) * SUB, :] = 1.0 - (((w[0] + w[1]) + w[2]) + w[3])
            for i in range(4):
                weights[i + 1, c, r * SUB : (r + 1) * SUB, :] = w[i]
        here, over = follow, under

    for copy in copies:
        copy.wait()
    start = lax.fori_loop(0, mine, lambda i, total: total + steps[i], jnp.int32(0))
    count = steps[mine]
    for i in range(steps.shape[0]):
        value = steps[i].astype(F32) * (1.0 / (4.0 * CSUB))
        factors[i : i + 1, :] = jnp.full((1, LANES), value, F32)
    sweep(state, spare, weights, force, count, tiles, strip_tiles, lambda t: waveform[start + t])

    def give(read):
        for c in range(tiles):
            for r in range(strip_tiles):
                relaxed[r * SUB : (r + 1) * SUB, cols(c)] = read(r, c)

        @pl.when(odd)
        def _():
            for c in range(tiles):
                for r in range(HT):
                    edge_a[r * SUB : (r + 1) * SUB, cols(c)] = read(r, c)
                    edge_b[r * SUB : (r + 1) * SUB, cols(c)] = read(strip_tiles - HT + r, c)

        @pl.when(jnp.logical_not(odd))
        def _():
            for c in range(tiles):
                for r in range(HT):
                    edge_b[r * SUB : (r + 1) * SUB, cols(c)] = read(r, c)
                    edge_a[r * SUB : (r + 1) * SUB, cols(c)] = read(strip_tiles - HT + r, c)

    last = mine == lax.axis_size("tm") - 1

    @pl.when(last)
    def _():
        give(lambda r, c: initial[r * SUB : (r + 1) * SUB, cols(c)])

    @pl.when(jnp.logical_not(last))
    def _():
        give(lambda r, c: state[c, PAD + HALO + r * SUB : PAD + HALO + (r + 1) * SUB, :])


def second_body(
    relaxed, edge_a, edge_b, point, got_a, got_b, weights, steps_far, coarse, state, spare, tmp, steps, sems
):
    copies = fetch(((steps_far, steps),), sems)
    rows, width = point.shape
    tiles, strip_tiles = width // LANES, rows // SUB
    mine, strip = lax.axis_index("tm"), lax.axis_index("space")
    odd = lax.rem(strip, 2) == 1
    for c in range(tiles):
        for r in range(strip_tiles):
            at = slice(r * SUB, (r + 1) * SUB)
            to = PAD + HALO + r * SUB
            state[c, to : to + SUB, :] = relaxed[at, cols(c)] - point[at, cols(c)]
        for at in (0, HALO + rows + HALO - SUB):
            tmp[c, at : at + SUB, :] = jnp.zeros((SUB, LANES), F32)

    def place(pair, above):
        edge, payload = pair
        unpack(tmp, tiles, rows, payload, above, 0)
        base = 0 if above else HALO + rows
        for c in range(tiles):
            for r in range(HT):
                at = base + r * SUB
                state[c, PAD + at : PAD + at + SUB, :] = edge[r * SUB : (r + 1) * SUB, cols(c)] - tmp[c, at : at + SUB, :]

    with_halos(odd, (edge_a, got_a), (edge_b, got_b), place)
    copies[0].wait()
    count = steps[mine]
    sweep(state, spare, weights, None, count, tiles, strip_tiles, None)
    pairs = halve()
    for c in range(tiles // 2):
        wide = [row_pairs(state, (2 * c + k,), PAD + HALO, rows // 2) for k in (0, 1)]
        coarse[:, cols(c)] = 0.25 * dot(jnp.concatenate(wide, axis=1), pairs)


def assemble_body(strips, fields, total, weights, conduct):
    count = len(strips)
    rows, width = strips[0].shape
    tiles = width // LANES
    mine = lax.axis_index("space")
    per_block = BLK_R // 2
    zero = jnp.zeros((SUB, LANES), F32)
    for c in range(tiles):
        conduct[c, 0:PAD, :] = zero
        conduct[c, PAD + count * rows :, :] = zero
    for k in range(count):
        base = (mine ^ k) * rows
        for c in range(tiles):
            for r in range(rows // SUB):
                to = pl.multiple_of(base + r * SUB, SUB)
                total[c, pl.ds(to, SUB), :] = strips[k][r * SUB : (r + 1) * SUB, cols(c)]
                weights[0, c, pl.ds(to, SUB), :] = fields[k][c * rows + r * SUB : c * rows + (r + 1) * SUB, :]
                block = tiles * rows + c * (rows // per_block) + r * (SUB // per_block)
                two = [jnp.broadcast_to(fields[k][block + i : block + i + 1, :], (SUB, LANES)) for i in (0, 1)]
                conduct[c, pl.ds(PAD + to, SUB), :] = jnp.where(iota(0) < per_block, two[0], two[1])
    for r in range(count * rows // SUB):
        at = PAD + r * SUB
        here = [conduct[c, at : at + SUB, :] for c in range(tiles)]
        for c in range(tiles):
            left, right = beside(here, c, zero)
            above = conduct[c, at - 1 : at + SUB - 1, :]
            below = conduct[c, at + 1 : at + SUB + 1, :]
            own = weights[0, c, r * SUB : (r + 1) * SUB, :]
            w = [own * jnp.sqrt(here[c] * other) for other in (above, below, left, right)]
            weights[0, c, r * SUB : (r + 1) * SUB, :] = ((w[0] + w[1]) + w[2]) + w[3]
            for k in range(4):
                weights[k + 1, c, r * SUB : (r + 1) * SUB, :] = w[k]


def link(buffers, weights, factor):
    state, one, two = buffers
    tiles, padded, _ = state.shape

    def step(source, target):
        for r in range((padded - 2 * PAD) // SUB):
            at = PAD + r * SUB
            here = [source[c, at : at + SUB, :] for c in range(tiles)]
            for c in range(tiles):
                left, right = beside(here, c)
                above = source[c, at - 1 : at + SUB - 1, :]
                below = source[c, at + 1 : at + SUB + 1, :]
                w = [weights[k, c, r * SUB : (r + 1) * SUB, :] for k in range(5)]
                change = (w[1] * above + w[2] * below) + (w[3] * left + w[4] * right) - w[0] * here[c]
                target[c, at : at + SUB, :] = here[c] + factor * change

    source = state
    for k in range(CSUB):
        target = state if k == CSUB - 1 else (two if source is one else one)
        step(source, target)
        source = target


def scan_body(stage, final, refs):
    total, got, before, weights, factors = refs[:5]
    tiles, height, _ = total.shape
    size = 1 << stage
    mine, strip = lax.axis_index("tm"), lax.axis_index("space")
    upper = lax.rem(mine // size, 2) == 1
    first = (mine // (2 * size)) * (2 * size) + size
    if final:
        relaxed, out, *buffers, errors, tmp = refs[5:]
        rows = 2 * relaxed.shape[0] // 4
    else:
        total_out, errors, *buffers = refs[5:]
        rows = errors.shape[1]
    mine_rows = pl.multiple_of(strip * rows, SUB)
    zero = jnp.zeros((SUB, LANES), F32)
    state = buffers[0]
    for c in range(tiles):
        for buffer in buffers:
            buffer[c, 0:PAD, :] = zero
            buffer[c, PAD + height :, :] = zero

    def load(ref):
        for c in range(tiles):
            for r in range(height // SUB):
                state[c, PAD + r * SUB : PAD + (r + 1) * SUB, :] = ref[c, r * SUB : (r + 1) * SUB, :]

    @pl.when(upper)
    def _():
        load(got)

    @pl.when(jnp.logical_not(upper))
    def _():
        load(total)

    def keep():
        for c in range(tiles):
            piece = state[c, pl.ds(PAD + mine_rows, rows), :]
            errors[c, :, :] = piece if before is None else before[c, :, :] + piece

    def pass_on():
        for c in range(tiles):
            if before is None:
                errors[c, :, :] = jnp.zeros((rows, LANES), F32)
            else:
                errors[c, :, :] = before[c, :, :]

    pass_on()

    def turn(i, _):
        @pl.when(jnp.logical_and(upper, first + i == mine))
        def _():
            keep()

        link(buffers, weights, jnp.broadcast_to(factors[pl.ds(first + i, 1), :], (SUB, LANES)))

    if final:
        turns = jnp.where(upper, mine - first, 0)
        lax.fori_loop(0, turns, turn, None)

        @pl.when(upper)
        def _():
            keep()

        pairs = double()
        for c in range(tiles):
            wide = dot(errors[c, :, :], pairs)
            for k in (0, 1):
                part = wide[:, k * LANES : (k + 1) * LANES]
                tmp[2 * c + k, pl.ds(0, rows, stride=2), :] = part
                tmp[2 * c + k, pl.ds(1, rows, stride=2), :] = part
        for c in range(2 * tiles):
            out[:, cols(c)] = relaxed[:, cols(c)] + tmp[c, :, :]
    else:
        lax.fori_loop(0, size, turn, None)

        def close(ref):
            for c in range(tiles):
                for r in range(height // SUB):
                    at = slice(r * SUB, (r + 1) * SUB)
                    total_out[c, at, :] = ref[c, at, :] + state[c, PAD + r * SUB : PAD + (r + 1) * SUB, :]

        @pl.when(upper)
        def _():
            close(total)

        @pl.when(jnp.logical_not(upper))
        def _():
            close(got)


def shards(point_states, initial_state, node_rate, source_map, waveform, cond_table, class_map, interval_steps):
    assert point_states.shape[0] == 1
    intervals, strips = lax.axis_size("tm"), lax.axis_size("space")
    assert intervals & (intervals - 1) == 0 and strips & (strips - 1) == 0
    point = point_states[0]
    rows, width = point.shape
    tiles, ctiles, crows, blocks = width // LANES, width // LANES // 2, rows // 2, rows // BLK_R
    height, cheight = rows + 2 * HALO, crows * strips
    packed = -(-(3 * STEP_MOST + HT) // SUB) * SUB
    fields_rows = -(-ctiles * (crows + blocks) // SUB) * SUB
    both = ("tm", "space")

    def side(s, which):
        other = s ^ 1 if which == "a" else (s + 1 if s % 2 else s - 1)
        return other if 0 <= other < strips else None

    def exchange(value, ahead, move):
        pairs = []
        for j in range(intervals):
            for s in range(strips):
                to = move(s)
                if to is not None:
                    pairs.append((j * strips + s, ((j + ahead) % intervals) * strips + to))
        return lax.ppermute(value, both, pairs)

    strip = f32(rows, width)
    pay_a, pay_b, own_blocks, point, rate, source, initial = call(
        pack_body, [FAR] * 6,
        (f32(packed, width), f32(packed, width), f32(SUB, width), strip, strip, strip, strip),
        [
            pltpu.SMEM(cond_table.shape, F32),
            pltpu.SMEM(class_map.shape, jnp.int32),
            pltpu.SemaphoreType.DMA((6,)),
        ],
        1 << 20,
    )(*[far(x) for x in (point, node_rate, source_map, initial_state, cond_table, class_map)])
    got_a = exchange(pay_a, 0, lambda s: side(s, "a"))
    got_b = exchange(pay_b, 0, lambda s: side(s, "b"))
    field = call(
        coarsen_body, [VM] * 2, f32(fields_rows, LANES), [pltpu.VMEM((tiles, rows, LANES), F32)], 1 << 20
    )(rate, own_blocks)
    fields = [field]
    for k in range(1, strips):
        fields.append(exchange(field, 0, lambda s, k=k: s ^ k))

    grid = pltpu.VMEM((tiles, height + 2 * PAD, LANES), F32)
    flat = pltpu.VMEM((tiles, height, LANES), F32)
    steps_near = pltpu.SMEM(interval_steps.shape, jnp.int32)
    passed, edge_a, edge_b, weights, factors = call(
        first_body, [VM] * 7 + [FAR] * 2,
        (strip, f32(HALO, width), f32(HALO, width), f32(5, tiles, height, LANES), f32(-(-intervals // SUB) * SUB, LANES)),
        [grid, grid, flat, flat, flat, steps_near, pltpu.SMEM(waveform.shape, F32), pltpu.SemaphoreType.DMA((2,))],
        1 << 24,
    )(point, rate, source, got_a, got_b, initial, own_blocks, far(interval_steps), far(waveform))
    relaxed = exchange(passed, 1, lambda s: s)
    edge_a = exchange(edge_a, 1, lambda s: side(s, "a"))
    edge_b = exchange(edge_b, 1, lambda s: side(s, "b"))

    change = call(
        second_body, [VM] * 7 + [FAR], f32(crows, width // 2),
        [grid, grid, flat, steps_near, pltpu.SemaphoreType.DMA((1,))],
        1 << 24,
    )(relaxed, edge_a, edge_b, point, got_a, got_b, weights, far(interval_steps))
    changes = [change]
    for k in range(1, strips):
        changes.append(exchange(change, 0, lambda s, k=k: s ^ k))

    def assemble(*refs):
        assemble_body(refs[:strips], refs[strips : 2 * strips], *refs[2 * strips :])

    total, coarse_weights = call(
        assemble, [VM] * (2 * strips), (f32(ctiles, cheight, LANES), f32(5, ctiles, cheight, LANES)),
        [pltpu.VMEM((ctiles, cheight + 2 * PAD, LANES), F32)], 1 << 20,
    )(*changes, *fields)

    errors = None
    stages = intervals.bit_length() - 1
    for stage in range(stages):
        got = lax.ppermute(total, "tm", [(j, j ^ (1 << stage)) for j in range(intervals)])
        final = stage == stages - 1
        some = errors is not None

        def body(*refs, stage=stage, final=final, some=some):
            refs = refs if some else (*refs[:2], None, *refs[2:])
            scan_body(stage, final, refs)

        buffers = [pltpu.VMEM((ctiles, cheight + 2 * PAD, LANES), F32)] * 3
        lead = [total, got] + ([errors] if some else []) + [coarse_weights, factors]
        specs = [VM] * len(lead)
        if final:
            out = call(
                body, specs + [VM], f32(rows, width),
                buffers + [pltpu.VMEM((ctiles, crows, LANES), F32), pltpu.VMEM((tiles, rows, LANES), F32)], 1 << 23,
            )(*lead, relaxed)
        else:
            total, errors = call(
                body, specs, (f32(ctiles, cheight, LANES), f32(ctiles, crows, LANES)), buffers, 1 << 23
            )(*lead)
    return out[None]


def solution(mesh):
    placed = (
        P("tm", "space", None),
        P("space", None),
        P("space", None),
        P("space", None),
        P(),
        P(),
        P("space", None),
        P(),
    )

    return jax.shard_map(shards, mesh=mesh, in_specs=placed, out_specs=P("tm", "space", None), check_vma=False)
```
